32 devices in a mesh: groups: 2 (over y), band: 4 (over z), inl: 2 (over x), xl: 2 (over core).
Axes of the slice: x: 2, y: 2, z: 4, core: 2. Of those that a mesh axis runs over, the one named last changes fastest.
Arguments:
- traces: float32 [32, 256, 2048], P(('groups', 'inl', 'xl'), 'band'), parts along dimension 0, may hold values from -6 to 6
- band_start: int32 [64], replicated, may hold values from 0 to 832
- taper_len: int32 [64], replicated, may hold values from 1 to 64
- band_weight: float32 [64], replicated, may hold values from 0.02 to 0.2
- labels: int32 [32, 256], P(('groups', 'inl', 'xl')), parts along dimension 0, may hold values 0 or 1
Outputs:
- fault_map: float32 [32, 16, 256], P(('groups', 'band'), ('inl', 'xl')), parts along dimension 0
- misfit: float32 [32, 16, 256], P(('groups', 'band'), ('inl', 'xl')), parts along dimension 0
The draws below stay inside these ranges and needn't reach their ends.
There are 2 independent parts, one for each index of `groups`. The reference program is written for one: setup_inputs(seed, part) draws one part's arguments, and reference() takes and returns one part's arrays. A program takes and returns all parts, laid end to end along the dimension named above; an argument that names none is the same for every part. Nothing has to cross between parts.
All inputs are finite; a program needn't handle non-finite values. No bound on the sum of `labels` on one device may be relied on, other than what follows from the above.
Results may differ from the reference program's by a relative error of at most 0.0003.
Values may be sent and summed in bfloat16 or wider, within the bound.
A program may use at most 64 MiB of HBM per device.

```python
import math
import jax
import jax.numpy as jnp
from jax import lax

NT = 2048
WIN = 256
HOP = 64
FR = 16
NB = 64
RAD_INL = 2
RAD_XL = 4
NI = 16
NX = 256


def place_ends(array, stream_key, least, largest):
    longest = array.shape.index(max(array.shape))
    spots = []
    for shift in (0, 1):
        where = [jax.random.randint(jax.random.fold_in(stream_key, axis), (), 0, length) for axis, length in enumerate(array.shape)]
        where[longest] = (where[longest] + shift) % array.shape[longest]
        spots.append(tuple(where))
    return array.at[spots[0]].set(least).at[spots[1]].set(largest)


def levels(rng, extent, split, smallest, high):
    def one(dim, blocks):
        steps = jax.random.uniform(jax.random.fold_in(jax.random.fold_in(rng, 6), dim), (blocks,), jnp.float32, smallest / len(split), high / len(split))
        return jnp.repeat(jnp.exp(steps), extent[dim] // blocks).reshape((-1,) + (1,) * (len(extent) - dim - 1))

    level = one(*split[0])
    for cut in split[1:]:
        level = level * one(*cut)
    return level


def scatter_about(stream_key, shape, scale, most, split=(), kind=jnp.bfloat16):
    entries = scale * jax.random.normal(stream_key, shape, jnp.float32)
    if split:
        entries = entries * levels(stream_key, shape, split, -0.22, 0.18)
    return jnp.clip(entries, -most, most).astype(kind)


def setup_inputs(seed: int = 0, part: int = 0) -> dict:
    key_list = jax.random.split(jax.random.key(seed), 6)
    part_splits = jax.random.split(jax.random.fold_in(key_list[5], part), 6)
    traces = scatter_about(part_splits[0], (NI, NX, NT), 1.0, 6.0, ((0, 4), (1, 4)), jnp.float32)
    band_start = place_ends(jax.random.randint(key_list[1], (NB,), 0, NT - (FR - 1) * HOP - WIN + 1), jax.random.fold_in(key_list[1], 1), 0, NT - (FR - 1) * HOP - WIN).astype(jnp.int32)
    taper_len = place_ends(jax.random.randint(key_list[2], (NB,), 1, WIN // 4 + 1), jax.random.fold_in(key_list[2], 1), 1, (WIN // 4 + 1) - 1).astype(jnp.int32)
    band_weight = jnp.clip(jnp.exp(jax.random.uniform(key_list[3], (NB,), jnp.float32, math.log(0.02), math.log(0.2))), 0.02, 0.2)
    labels = place_ends((jax.random.randint(part_splits[4], (NI, NX), 0, 4) < 1).astype(jnp.int32), jax.random.fold_in(part_splits[4], 1), 0, 1)
    return {"traces": traces, "band_start": band_start, "taper_len": taper_len, "band_weight": band_weight, "labels": labels}


epsilon = 1e-6


def wave_values(offsets, band_ids, taper_lens):
    shifted = offsets.astype(jnp.float32)
    ramp_len = taper_lens.astype(jnp.float32) + 1.0
    tapers = jnp.minimum(jnp.minimum((shifted + 1.0) / ramp_len, (WIN - shifted) / ramp_len), 1.0)
    cycles = ((band_ids + 1) * offsets) % WIN
    angles = cycles.astype(jnp.float32) * (2.0 * math.pi / WIN)
    return tapers * jnp.cos(angles), tapers * jnp.sin(angles)


def cross_box(values):
    padded = jnp.pad(values, [(0, 0)] * (values.ndim - 1) + [(RAD_XL, RAD_XL)])
    width = values.shape[-1]
    summed = padded[..., 0:width]
    for offset in range(1, 2 * RAD_XL + 1):
        summed = summed + padded[..., offset:offset + width]
    return summed


def coherence(s_ii, s_ix, s_xx):
    return ((s_ii - s_xx) ** 2 + 4.0 * s_ix ** 2) / (s_ii + s_xx + epsilon) ** 2


def band_partial(conc_band, weight):
    field_f32 = conc_band.astype(jnp.float32)
    padded = jnp.pad(field_f32, ((0, 0), (1, 1), (1, 1)))
    grad_in = 0.5 * (padded[:, 2:, 1:-1] - padded[:, :-2, 1:-1])
    grad_xl = 0.5 * (padded[:, 1:-1, 2:] - padded[:, 1:-1, :-2])
    smoothed = []
    for product in (grad_in * grad_in, grad_in * grad_xl, grad_xl * grad_xl):
        rows_pad = jnp.pad(product, ((0, 0), (RAD_INL, RAD_INL), (0, 0)))
        inline_sum = rows_pad[:, 0:NI]
        for offset in range(1, 2 * RAD_INL + 1):
            inline_sum = inline_sum + rows_pad[:, offset:offset + NI]
        smoothed.append(cross_box(inline_sum))
    return weight * (1.0 - coherence(smoothed[0], smoothed[1], smoothed[2]))


def reference(traces, band_start, taper_len, band_weight, labels):
    traces_bf = traces.astype(jnp.bfloat16)
    sample_lags = jnp.arange(WIN, dtype=jnp.int32)
    frame_ids = jnp.arange(FR, dtype=jnp.int32)

    def one_band(inputs):
        band_id, start_at, taper_one = inputs
        cosine, sine_part = wave_values(sample_lags, band_id, taper_one)
        kernel = jnp.stack([cosine, sine_part]).astype(jnp.bfloat16).astype(jnp.float32)
        time_ids = (start_at + frame_ids[:, None] * HOP + sample_lags[None, :]).astype(jnp.int32)

        def one_inline(trace_rows):
            frames = trace_rows[:, time_ids].astype(jnp.float32)
            coeffs = jnp.einsum("xfk,ck->cfx", frames, kernel, precision=lax.Precision.HIGHEST)
            return coeffs[0] ** 2 + coeffs[1] ** 2

        band_power = lax.map(one_inline, traces_bf)
        return jnp.log(1.0 + band_power)

    amplitude = lax.map(one_band, (jnp.arange(NB, dtype=jnp.int32), band_start.astype(jnp.int32), taper_len.astype(jnp.int32)))
    amplitude = amplitude.transpose(0, 2, 1, 3)
    average = jnp.mean(amplitude, axis=0, keepdims=True)
    concentration = (amplitude / (1.0 + average)).astype(jnp.bfloat16)

    def add_band(running, inputs):
        conc_band, weight = inputs
        return running + band_partial(conc_band, weight), None

    fault_map, unused = lax.scan(add_band, jnp.zeros((FR, NI, NX), jnp.float32), (concentration, band_weight))
    misfit = (jnp.tanh(fault_map) - labels.astype(jnp.float32)[None]) ** 2
    return fault_map, misfit
```

```python
import functools
import math

import jax
import jax.numpy as jnp
from jax import lax
from jax.experimental import pallas as pl
from jax.experimental.pallas import tpu as pltpu
from jax.sharding import PartitionSpec as P

WIN = 256
HOP = 64
FR = 16
NB = 64
RAD_INL = 2
RAD_XL = 4


epsilon = 1e-06


def with_halo(cells, sides, width):
    for axis, dim in sides:
        count = lax.axis_size(axis)
        ends = count - 1
        head = lax.slice_in_dim(cells, 0, width, axis=dim)
        tail = lax.slice_in_dim(cells, cells.shape[dim] - width, cells.shape[dim], axis=dim)
        cells = jnp.concatenate(
            [
                lax.ppermute(tail, axis, [(i, (i + 1) % count) for i in range(ends)]),
                cells,
                lax.ppermute(head, axis, [((i + 1) % count, i) for i in range(ends)]),
            ],
            axis=dim,
        )
    return cells


def wave_values(offsets, band_ids, taper_lens):
    shifted = offsets.astype(jnp.float32)
    ramp_len = taper_lens.astype(jnp.float32) + 1.0
    tapers = jnp.minimum(jnp.minimum((shifted + 1.0) / ramp_len, (WIN - shifted) / ramp_len), 1.0)
    cycles = (band_ids + 1) * offsets % WIN
    angles = cycles.astype(jnp.float32) * (2.0 * math.pi / WIN)
    return (tapers * jnp.cos(angles), tapers * jnp.sin(angles))


def band_coeffs(trace_rows, band_start, taper_len):
    row_total = trace_rows.shape[0]
    samples = trace_rows.shape[1]
    per_group = 8
    time_ids = jnp.arange(samples, dtype=jnp.int32)
    frame_ids = jnp.arange(FR, dtype=jnp.int32)

    def one_group(inputs):
        starts, tapers_in, band_ids = inputs
        offsets = time_ids[None, None, :] - starts[:, None, None] - frame_ids[None, :, None] * HOP
        valid = (offsets >= 0) & (offsets < WIN)
        clipped = jnp.clip(offsets, 0, WIN - 1)
        cosine, sine_part = wave_values(clipped, band_ids[:, None, None], tapers_in[:, None, None])
        kernel = jnp.stack([cosine, sine_part], axis=1)
        kernel = jnp.where(valid[:, None], kernel, 0.0).astype(jnp.bfloat16)
        kernel = kernel.reshape(per_group * 2 * FR, samples)
        return lax.dot_general(
            kernel, trace_rows, (((1,), (1,)), ((), ())), preferred_element_type=jnp.float32
        )

    group_count = NB // per_group
    grouped = lax.map(
        one_group,
        (
            band_start.reshape(group_count, per_group),
            taper_len.reshape(group_count, per_group),
            jnp.arange(NB, dtype=jnp.int32).reshape(group_count, per_group),
        ),
    )
    return grouped.reshape(NB, 2, FR, row_total)


def coherence(s_ii, s_ix, s_xx):
    return ((s_ii - s_xx) ** 2 + 4.0 * s_ix**2) / (s_ii + s_xx + epsilon) ** 2


def column_work(conc_block, band_weight):
    xl_cols = conc_block.shape[3]
    row_count = conc_block.shape[2]
    extended = with_halo(conc_block, (("band", 3),), RAD_XL + 1)
    field_f32 = extended.astype(jnp.float32)
    rows_pad = jnp.pad(field_f32, ((0, 0), (0, 0), (1, 1), (0, 0)))
    grad_in = 0.5 * (rows_pad[:, :, 2:, 1:-1] - rows_pad[:, :, :-2, 1:-1])
    grad_xl = 0.5 * (field_f32[..., 2:] - field_f32[..., :-2])
    col_count = grad_xl.shape[3]
    global_cols = lax.axis_index("band") * xl_cols - RAD_XL + jnp.arange(col_count, dtype=jnp.int32)
    inside = ((global_cols >= 0) & (global_cols < xl_cols * lax.axis_size("band"))).astype(
        jnp.float32
    )
    grad_in = grad_in * inside
    grad_xl = grad_xl * inside
    smoothed = []
    for product in (grad_in * grad_in, grad_in * grad_xl, grad_xl * grad_xl):
        inl_pad = jnp.pad(product, ((0, 0), (0, 0), (RAD_INL, RAD_INL), (0, 0)))
        inline_sum = inl_pad[:, :, 0:row_count]
        for offset in range(1, 2 * RAD_INL + 1):
            inline_sum = inline_sum + inl_pad[:, :, offset : offset + row_count]
        summed = inline_sum[..., 0:xl_cols]
        for offset in range(1, 2 * RAD_XL + 1):
            summed = summed + inline_sum[..., offset : offset + xl_cols]
        smoothed.append(summed)
    scores = band_weight[:, None, None, None] * (
        1.0 - coherence(smoothed[0], smoothed[1], smoothed[2])
    )
    return jnp.sum(scores, axis=0)


def on_device(traces, band_start, taper_len, band_weight, labels):
    il_rows, xl_cols, samples = traces.shape
    trace_rows = traces.reshape(il_rows * xl_cols, samples).astype(jnp.bfloat16)
    coeffs = band_coeffs(trace_rows, band_start, taper_len)
    coeffs = coeffs.reshape(NB, 2, FR, il_rows, xl_cols)
    band_power = coeffs[:, 0] ** 2 + coeffs[:, 1] ** 2
    amplitude = jnp.log(1.0 + band_power)
    average = jnp.mean(amplitude, axis=0, keepdims=True)
    concentration = (amplitude / (1.0 + average)).astype(jnp.bfloat16)
    spread = lax.all_to_all(concentration, ("inl", "xl"), split_axis=1, concat_axis=2, tiled=True)
    partial_cols = column_work(spread, band_weight)
    by_slab = lax.all_to_all(partial_cols, ("inl", "xl"), split_axis=1, concat_axis=0, tiled=True)
    fault_map = lax.all_to_all(by_slab, "band", split_axis=0, concat_axis=2, tiled=True)
    misfit = (jnp.tanh(fault_map) - labels.astype(jnp.float32)[None]) ** 2
    return (fault_map, misfit)


MESH = pl.DeviceIdType.MESH
EDGE = 16
PAD = 8
CHUNK = 512
HALO = RAD_XL + 1


def wave_block(first, start, taper, rows):
    lane = lax.broadcasted_iota(jnp.int32, (rows, 2 * NB), 1)
    time = lax.broadcasted_iota(jnp.int32, (rows, 2 * NB), 0) + first
    late = (lane >= NB).astype(jnp.int32)
    band = lane - late * NB
    lag = time - (start & 127) - late * HOP
    valid = (lag >= 0) & (lag < WIN)
    lag_f = lag.astype(jnp.float32)
    tapers = jnp.minimum(
        jnp.minimum(lag_f + 1.0, WIN - lag_f) / (taper.astype(jnp.float32) + 1.0), 1.0
    )
    tapers = jnp.where(valid, tapers, 0.0)
    cycles = ((band + 1) * lag) & (WIN - 1)
    quarter = (cycles + 32) >> 6
    x = (cycles - quarter * 64).astype(jnp.float32) * (2.0 * math.pi / WIN)
    z = x * x
    sin_x = x + x * z * (-1.6666654611e-1 + z * (8.3321608736e-3 + z * -1.9515295891e-4))
    cos_x = (1.0 - 0.5 * z) + z * z * (
        4.166664568298827e-2 + z * (-1.388731625493765e-3 + z * 2.443315711809948e-5)
    )
    swap = (quarter & 1) == 1
    cos_sign = jnp.where(((quarter + 1) & 2) == 2, -tapers, tapers)
    sin_sign = jnp.where((quarter & 2) == 2, -tapers, tapers)
    cosine = cos_sign * jnp.where(swap, sin_x, cos_x)
    sine = sin_sign * jnp.where(swap, cos_x, sin_x)
    return cosine.astype(jnp.bfloat16), sine.astype(jnp.bfloat16)


def split_bf16(x):
    high = x.astype(jnp.bfloat16)
    return high, (x - high.astype(jnp.float32)).astype(jnp.bfloat16)


def dot32(a, b):
    return jnp.dot(a, b, preferred_element_type=jnp.float32)


def twice(x):
    return jnp.concatenate([x, x], axis=1)


def fused_kernel(
    slabs, n_band, traces, start_ref, taper_ref, weight_ref, fault_ref,
    t32, tb, start_at, taper_at, weight_at,
    waves, power, field, packed, halo, corner, prods, part_out, part_in,
    load_sem, small_sem, main_send, main_recv, left_send, left_recv, right_send, right_recv,
    cross_send, cross_recv, cross_left_send, cross_left_recv, cross_right_send,
    cross_right_recv, part_send, part_recv,
):
    group = lax.axis_index("groups")
    beta = lax.axis_index("band")
    n_xl = lax.axis_size("xl")
    inl = lax.axis_index("inl")
    core = lax.axis_index("xl")
    slab = inl * n_xl + core
    il_rows, xl_cols = traces.shape[0], traces.shape[1]
    rows = il_rows * xl_cols

    def device(band_at, slab_at):
        return (group, band_at, slab_at // n_xl, slab_at % n_xl)

    smalls = [
        pltpu.make_async_copy(source, to, small_sem.at[i])
        for i, (source, to) in enumerate(
            (
                (start_ref, start_at),
                (taper_ref, taper_at),
                (weight_ref, weight_at),
            )
        )
    ]
    for small in smalls:
        small.start()
    loads = [
        pltpu.make_async_copy(
            traces.at[:, :, pl.ds(i * CHUNK, CHUNK)],
            t32.at[:, :, pl.ds(i * CHUNK, CHUNK)],
            load_sem.at[i],
        )
        for i in range(traces.shape[2] // CHUNK)
    ]
    for load in loads:
        load.start()

    barrier = pltpu.get_barrier_semaphore()
    for db in range(n_band):
        for ds in range(slabs):
            if db or ds:
                pl.semaphore_signal(
                    barrier,
                    inc=1,
                    device_id=device((beta + db) % n_band, (slab + ds) % slabs),
                    device_id_type=MESH,
                )

    for small in smalls:
        small.wait()
    start = twice(start_at[...])
    taper = twice(taper_at[...])
    for first in range(0, 512, 64):
        cosine, sine = wave_block(first, start, taper, 64)
        waves[first : first + 64, 0 : 2 * NB] = cosine
        waves[first : first + 64, 2 * NB : 4 * NB] = sine

    field[0:2, 3 + 9 * inl] = jnp.zeros((2,) + field.shape[2:], field.dtype)
    @pl.when(beta == 0)
    def _():
        halo[:, :, 0] = jnp.zeros((2, n_xl) + halo.shape[3:], halo.dtype)
        corner[:, 0] = jnp.zeros((2,) + corner.shape[2:], corner.dtype)

    @pl.when(beta == n_band - 1)
    def _():
        halo[:, :, 1] = jnp.zeros((2, n_xl) + halo.shape[3:], halo.dtype)
        corner[:, 1] = jnp.zeros((2,) + corner.shape[2:], corner.dtype)

    for row in range(2):
        prods[:, :, 2 + row + 10 * inl] = jnp.zeros((2, 3) + prods.shape[3:], jnp.float32)

    samples = traces.shape[2]
    tb[:, samples:] = jnp.zeros((rows, 128), jnp.bfloat16)

    def land(chunk):
        loads[chunk].wait()
        span = slice(chunk * CHUNK, (chunk + 1) * CHUNK)
        tb[:, span] = t32[:, :, span].reshape(rows, CHUNK).astype(jnp.bfloat16)

    def one_step(step):
        if step % 4 == 1 and step < 13:
            land(step // 4 + 1)
        at = step * 128
        coeffs = dot32(tb[:, pl.ds(at, 512)], waves[...])
        cosine, sine = coeffs[:, 0 : 2 * NB], coeffs[:, 2 * NB :]
        power[step] = cosine * cosine + sine * sine

    land(0)

    first_step = start >> 7
    half_r = lax.broadcasted_iota(jnp.int32, (2 * NB, 2 * NB), 0) // NB
    half_c = lax.broadcasted_iota(jnp.int32, (2 * NB, 2 * NB), 1) // NB
    mean_mat = jnp.where(half_r == half_c, 1.0 / NB, 0.0).astype(jnp.bfloat16)

    def concentrations(m, slot):
        for j in range(2):
            pair = m * 2 + j
            chosen = power[pair]
            for q in range(1, 7):
                chosen = jnp.where(first_step == q, power[pair + q], chosen)
            amplitude = jnp.log(1.0 + chosen)
            high, low = split_bf16(amplitude)
            average = dot32(high, mean_mat) + dot32(low, mean_mat)
            value = (amplitude / (1.0 + average)).astype(jnp.bfloat16)
            field[slot, mine, middle, j * 2 * NB : (j + 1) * 2 * NB] = value.reshape(
                il_rows, xl_cols, 2 * NB
            )

    mine = pl.ds(4 + core * il_rows, il_rows)
    border_from = pl.ds(4 + core * il_rows + 1 - inl, 3)
    border_to = pl.ds(1 + 11 * inl, 3)
    at_border = core == 1 - inl
    middle = pl.ds(EDGE, xl_cols)
    first_cols, last_cols = pl.ds(EDGE, EDGE), pl.ds(xl_cols, EDGE)
    left_band, right_band = (beta + n_band - 1) % n_band, (beta + 1) % n_band
    has_left, has_right = beta > 0, beta < n_band - 1

    def place_of(m):
        owner, half = m % 2, m // 2
        return owner, half, half + 2 * ((core + owner) % 2)

    def one_hot(ones):
        return jnp.where(ones, 1.0, 0.0).astype(jnp.bfloat16)

    out_at = lax.broadcasted_iota(jnp.int32, (96, 8 * EDGE), 0)
    in_at = lax.broadcasted_iota(jnp.int32, (96, 8 * EDGE), 1)
    from_right = in_at // (4 * EDGE)
    in_row = in_at % (4 * EDGE) // EDGE
    in_col = in_at % EDGE - from_right * (EDGE - HALO)
    in_code = jnp.where(
        (in_col >= 0) & (in_col < HALO), from_right * 64 + in_row * HALO + in_col, -2
    )
    corner_code = jnp.where(
        out_at % 16 < 3 * HALO, out_at // 16 % 2 * 64 + out_at % 16 + (1 - inl) * HALO, -1
    )
    out_code = jnp.where(out_at < 64, out_at // 32 * 64 + out_at % 32, corner_code)
    pack_mat = one_hot(in_code == out_code)

    def unpack_matrix(depth, first):
        to = lax.broadcasted_iota(jnp.int32, (8 * EDGE, 2 * depth), 0)
        at = lax.broadcasted_iota(jnp.int32, (8 * EDGE, 2 * depth), 1)
        to_right = to // (4 * EDGE)
        col = to % EDGE - (1 - to_right) * (EDGE - HALO)
        code = (to % (4 * EDGE) // EDGE - first) * HALO + col
        return one_hot(
            (col >= 0) & (col < HALO) & (code == at % depth) & (to_right == at // depth)
        )

    unpack_mat = unpack_matrix(32, 0)
    unpack_corner = unpack_matrix(16, inl)

    def pack(m):
        _, _, slot = place_of(m)
        edges = jnp.concatenate(
            [
                field[slot, mine, first_cols].reshape(4 * EDGE, 4 * NB),
                field[slot, mine, last_cols].reshape(4 * EDGE, 4 * NB),
            ],
            axis=0,
        )
        packed[m] = dot32(pack_mat, edges).astype(jnp.bfloat16)

    def unpack(half, block, halves, matrix):
        edges = dot32(matrix, halves).astype(jnp.bfloat16)
        to = pl.ds(4 * block, 4)
        field[half, to, 0:EDGE] = edges[: 4 * EDGE].reshape(4, EDGE, 4 * NB)
        field[half, to, EDGE + xl_cols :] = edges[4 * EDGE :].reshape(4, EDGE, 4 * NB)

    sent = []

    def send(asked, source, to, send_sem, recv_sem, band_at, slab_at):
        copy = pltpu.make_async_remote_copy(
            src_ref=source,
            dst_ref=to,
            send_sem=send_sem,
            recv_sem=recv_sem,
            device_id=device(band_at, slab_at),
            device_id_type=MESH,
        )
        sent.append((asked, copy))

        @pl.when(asked)
        def _():
            copy.start()

    def send_rows(m):
        owner, half, slot = place_of(m)
        own_chip, other_chip = inl * n_xl + owner, (1 - inl) * n_xl + owner
        send(at_border, field.at[slot, border_from, middle], field.at[half, border_to, middle],
             cross_send.at[m], cross_recv.at[half], beta, other_chip)
        send(core == 1 - owner, field.at[slot, mine, middle], field.at[half, mine, middle],
             main_send.at[m], main_recv.at[half], beta, own_chip)

    def send_edges(m):
        owner, half, _ = place_of(m)
        own_chip, other_chip = inl * n_xl + owner, (1 - inl) * n_xl + owner
        send(at_border & has_left, packed.at[m, pl.ds(64, 16)], corner.at[half, 1],
             cross_left_send.at[m], cross_left_recv.at[half], left_band, other_chip)
        send(at_border & has_right, packed.at[m, pl.ds(80, 16)], corner.at[half, 0],
             cross_right_send.at[m], cross_right_recv.at[half], right_band, other_chip)
        send(has_left, packed.at[m, pl.ds(0, 32)], halo.at[half, core, 1],
             left_send.at[m], left_recv.at[half * 2 + core], left_band, own_chip)
        send(has_right, packed.at[m, pl.ds(32, 32)], halo.at[half, core, 0],
             right_send.at[m], right_recv.at[half * 2 + core], right_band, own_chip)

    for step in range(8):
        one_step(step)
    for m in range(4):
        if m:
            pack(m - 1)
        for step in range(8 + 2 * m, min(10 + 2 * m, 14)):
            one_step(step)
        concentrations(m, place_of(m)[2])
        if m:
            send_edges(m - 1)
        else:
            pl.semaphore_wait(barrier, n_band * slabs - 1)
        send_rows(m)
    pack(3)
    send_edges(3)

    wide = xl_cols + 2 * PAD
    cells = pl.ds(EDGE - PAD, wide)
    shape = (wide, xl_cols + 2 * EDGE)
    out_x = lax.broadcasted_iota(jnp.int32, shape, 0) + (EDGE - PAD)
    in_x = lax.broadcasted_iota(jnp.int32, shape, 1)
    diff_mat = (
        (in_x == out_x + 1).astype(jnp.float32) - (in_x == out_x - 1).astype(jnp.float32)
    ).astype(jnp.bfloat16)
    out_x = lax.broadcasted_iota(jnp.int32, (xl_cols, wide), 0)
    in_x = lax.broadcasted_iota(jnp.int32, (xl_cols, wide), 1) - PAD
    at_x = in_x + beta * xl_cols
    near = (jnp.abs(in_x - out_x) <= RAD_XL) & (at_x >= 0) & (at_x < xl_cols * n_band)
    box_mat = near.astype(jnp.float32).astype(jnp.bfloat16)
    box_twice = twice(box_mat)
    weights = twice(twice(weight_at[...]))
    row = lax.broadcasted_iota(jnp.int32, (16, 4 * NB), 0)
    lane = lax.broadcasted_iota(jnp.int32, (16, 4 * NB), 1)
    w_high, w_low = split_bf16(weights)
    w_high = w_high.astype(jnp.float32)
    w_low = w_low.astype(jnp.float32)
    weight_mat = jnp.where(
        row == lane // NB, w_high, jnp.where(row - 4 == lane // NB, w_low, 0.0)
    ).astype(jnp.bfloat16)

    def landed(block, sem):
        pltpu.make_async_remote_copy(
            src_ref=block,
            dst_ref=block,
            send_sem=main_send.at[0],
            recv_sem=sem,
            device_id=device(beta, inl * n_xl + 1 - core),
            device_id_type=MESH,
        ).wait_recv()

    def own_chip_landed(half):
        landed(
            field.at[half, pl.ds(4 + (1 - core) * il_rows, il_rows), middle], main_recv.at[half]
        )

        @pl.when(has_right)
        def _():
            for source in range(2):
                landed(halo.at[half, source, 1], left_recv.at[half * 2 + source])

        @pl.when(has_left)
        def _():
            for source in range(2):
                landed(halo.at[half, source, 0], right_recv.at[half * 2 + source])

        for source in range(2):
            halves = jnp.concatenate([halo[half, source, 0], halo[half, source, 1]], axis=0)
            unpack(half, 1 + source, halves, unpack_mat)

    def other_chip_landed(half):
        landed(field.at[half, pl.ds(12 - 11 * inl, 3), middle], cross_recv.at[half])

        @pl.when(has_right)
        def _():
            landed(corner.at[half, 1], cross_left_recv.at[half])

        @pl.when(has_left)
        def _():
            landed(corner.at[half, 0], cross_right_recv.at[half])

        halves = jnp.concatenate([corner[half, 0], corner[half, 1]], axis=0)
        unpack(half, 3 - 3 * inl, halves, unpack_corner)

    def one_product(half, turn):
        i = 4 + turn + inl * (7 - 2 * turn)
        grad_xl = dot32(diff_mat, field[half, i])
        grad_in = field[half, i + 1, cells].astype(jnp.float32) - field[
            half, i - 1, cells
        ].astype(jnp.float32)
        prods[half, 0, i] = grad_in * grad_in
        prods[half, 1, i] = grad_in * grad_xl
        prods[half, 2, i] = grad_xl * grad_xl

    parts = []

    def slab_scores(half, turn):
        place = turn + inl * (1 - 2 * turn)
        base = 2 + place * il_rows
        slot = turn * 2 + half
        sums = [[] for _ in range(il_rows)]
        for which in range(3):
            p = [prods[half, which, base + r] for r in range(8)]
            a, b, c = p[1] + p[2], p[5] + p[6], p[3] + p[4]
            ac, bc = a + c, b + c
            for r, total in enumerate((p[0] + ac, p[5] + ac, p[2] + bc, p[7] + bc)):
                high, low = split_bf16(total)
                sums[r].append(dot32(box_twice, jnp.concatenate([high, low], axis=0)))
        scores = []
        for s_ii, s_ix, s_xx in sums:
            total = s_ii + s_xx + 4.0 * epsilon
            gap = s_ii - s_xx
            scores.append(1.0 - (gap * gap + 4.0 * (s_ix * s_ix)) / (total * total))
        high, low = split_bf16(jnp.concatenate(scores, axis=0))
        nt = (((1,), (1,)), ((), ()))
        both = lax.dot_general(
            weight_mat, high, nt, preferred_element_type=jnp.float32
        ) + lax.dot_general(weight_mat, low, nt, preferred_element_type=jnp.float32)
        both = both[0:8]
        both = both + pltpu.roll(both, 4, 0)
        upper = lax.broadcasted_iota(jnp.int32, (8, 128), 0) < 4
        part_out[slot] = jnp.where(upper, both[:, 0:128], both[:, 128:256])
        part = pltpu.make_async_remote_copy(
            src_ref=part_out.at[slot],
            dst_ref=part_in.at[beta],
            send_sem=part_send.at[slot],
            recv_sem=part_recv.at[beta],
            device_id=device(half * 2 + core, inl * n_xl + place),
            device_id_type=MESH,
        )
        own = (half * 2 + core == beta) & (place == core)
        parts.append((part, own))

        @pl.when(own)
        def _():
            part_in[beta] = part_out[slot]

        @pl.when(jnp.logical_not(own))
        def _():
            part.start()

    for half in range(2):
        own_chip_landed(half)
        for turn in range(7):
            one_product(half, turn)
        slab_scores(half, 0)
    for half in range(2):
        other_chip_landed(half)
        for turn in range(7, 10):
            one_product(half, turn)
        slab_scores(half, 1)

    for source in range(n_band):
        @pl.when(jnp.logical_not((beta % 2 == core) & (beta == source)))
        def _(source=source):
            pltpu.make_async_remote_copy(
                src_ref=part_out.at[0],
                dst_ref=part_in.at[source],
                send_sem=part_send.at[0],
                recv_sem=part_recv.at[source],
                device_id=device((beta + 1) % n_band, slab),
                device_id_type=MESH,
            ).wait_recv()

    for source in range(n_band):
        fault_ref[source] = part_in[source]

    for asked, copy in sent:
        @pl.when(asked)
        def _(copy=copy):
            copy.wait_send()

    for part, own in parts:
        @pl.when(jnp.logical_not(own))
        def _(part=part):
            part.wait_send()


def final_kernel(parts_ref, labels_ref, fault_ref, misfit_ref):
    first_half = lax.broadcasted_iota(jnp.int32, (8, 128), 1) < 64
    labels = labels_ref[...].astype(jnp.float32)
    halves = [[], []]
    for c in range(0, parts_ref.shape[0], 2):
        one, two = parts_ref[c], parts_ref[c + 1]
        halves[0].append(jnp.where(first_half, one, pltpu.roll(two, 64, 1)))
        halves[1].append(jnp.where(first_half, pltpu.roll(one, 64, 1), two))
    frames = fault_ref.shape[0]
    for odd in range(2):
        blocks = jnp.concatenate(halves[odd], axis=1)
        for two in range(2):
            i = two * 2 + odd
            here = blocks[two * 4 : two * 4 + 4]
            miss = jnp.tanh(here) - labels[i : i + 1]
            miss = miss * miss
            for f in range(frames):
                fault_ref[f, i : i + 1] = here[f : f + 1]
                misfit_ref[f, i : i + 1] = miss[f : f + 1]


def fused(traces, band_start, taper_len, band_weight, labels):
    il_rows, xl_cols, samples = traces.shape
    rows = il_rows * xl_cols
    n_band = lax.axis_size("band")
    slabs = lax.axis_size("inl") * lax.axis_size("xl")
    frames = FR // n_band
    out = jax.ShapeDtypeStruct((frames, il_rows, xl_cols * n_band), jnp.float32)
    vmem = pl.BlockSpec(memory_space=pltpu.VMEM)
    dma = pltpu.SemaphoreType.DMA
    parts = pl.pallas_call(
        functools.partial(fused_kernel, slabs, n_band),
        out_shape=jax.ShapeDtypeStruct((n_band, 8, 128), jnp.float32),
        in_specs=[pl.BlockSpec(memory_space=pltpu.HBM)] * 4,
        out_specs=vmem,
        scratch_shapes=[
            pltpu.VMEM((il_rows, xl_cols, samples), jnp.float32),
            pltpu.VMEM((rows, samples + 128), jnp.bfloat16),
            pltpu.VMEM((1, NB), jnp.int32),
            pltpu.VMEM((1, NB), jnp.int32),
            pltpu.VMEM((1, NB), jnp.float32),
            pltpu.VMEM((512, 4 * NB), jnp.bfloat16),
            pltpu.VMEM((14, rows, 2 * NB), jnp.float32),
            pltpu.VMEM((4, 16, xl_cols + 2 * EDGE, 4 * NB), jnp.bfloat16),
            pltpu.VMEM((4, 96, 4 * NB), jnp.bfloat16),
            pltpu.VMEM((2, 2, 2, 32, 4 * NB), jnp.bfloat16),
            pltpu.VMEM((2, 2, 16, 4 * NB), jnp.bfloat16),
            pltpu.VMEM((2, 3, 16, xl_cols + 2 * PAD, 4 * NB), jnp.float32),
            pltpu.VMEM((slabs, 8, 128), jnp.float32),
            pltpu.VMEM((n_band, 8, 128), jnp.float32),
            dma((samples // CHUNK,)),
            dma((3,)),
            dma((4,)),
            dma((2,)),
            dma((4,)),
            dma((4,)),
            dma((4,)),
            dma((4,)),
            dma((4,)),
            dma((2,)),
            dma((4,)),
            dma((2,)),
            dma((4,)),
            dma((2,)),
            dma((slabs,)),
            dma((n_band,)),
        ],
        compiler_params=pltpu.CompilerParams(
            collective_id=0, has_side_effects=True, vmem_limit_bytes=32 * 1024 * 1024
        ),
    )(
        *[
            pltpu.with_memory_space_constraint(operand, pltpu.HBM)
            for operand in (
                traces,
                band_start.reshape(1, NB),
                taper_len.reshape(1, NB),
                band_weight.reshape(1, NB),
            )
        ]
    )
    return pl.pallas_call(
        final_kernel, out_shape=(out, out), in_specs=[vmem, vmem], out_specs=(vmem, vmem)
    )(
        pltpu.with_memory_space_constraint(parts, pltpu.VMEM),
        pltpu.with_memory_space_constraint(labels, pltpu.VMEM),
    )


def solution(mesh):
    shape = mesh.shape
    square = shape["band"] == 4 and shape["inl"] == 2 and shape["xl"] == 2
    return jax.shard_map(
        fused if square else on_device,
        mesh=mesh,
        in_specs=(
            P(("groups", "inl", "xl"), "band", None),
            P(),
            P(),
            P(),
            P(("groups", "inl", "xl"), None),
        ),
        out_specs=(
            P(("groups", "band"), ("inl", "xl"), None),
            P(("groups", "band"), ("inl", "xl"), None),
        ),
        check_vma=False,
    )
```

```python
import functools
import math

import jax
import jax.numpy as jnp
from jax import lax
from jax.experimental import pallas as pl
from jax.experimental.pallas import tpu as pltpu
from jax.sharding import PartitionSpec as P

WIN = 256
HOP = 64
FR = 16
NB = 64
RAD_INL = 2
RAD_XL = 4


epsilon = 1e-06


def with_halo(cells, sides, width):
    for axis, dim in sides:
        count = lax.axis_size(axis)
        ends = count - 1
        head = lax.slice_in_dim(cells, 0, width, axis=dim)
        tail = lax.slice_in_dim(cells, cells.shape[dim] - width, cells.shape[dim], axis=dim)
        cells = jnp.concatenate(
            [
                lax.ppermute(tail, axis, [(i, (i + 1) % count) for i in range(ends)]),
                cells,
                lax.ppermute(head, axis, [((i + 1) % count, i) for i in range(ends)]),
            ],
            axis=dim,
        )
    return cells


def wave_values(offsets, band_ids, taper_lens):
    shifted = offsets.astype(jnp.float32)
    ramp_len = taper_lens.astype(jnp.float32) + 1.0
    tapers = jnp.minimum(jnp.minimum((shifted + 1.0) / ramp_len, (WIN - shifted) / ramp_len), 1.0)
    cycles = (band_ids + 1) * offsets % WIN
    angles = cycles.astype(jnp.float32) * (2.0 * math.pi / WIN)
    return (tapers * jnp.cos(angles), tapers * jnp.sin(angles))


def band_coeffs(trace_rows, band_start, taper_len):
    row_total = trace_rows.shape[0]
    samples = trace_rows.shape[1]
    per_group = 8
    time_ids = jnp.arange(samples, dtype=jnp.int32)
    frame_ids = jnp.arange(FR, dtype=jnp.int32)

    def one_group(inputs):
        starts, tapers_in, band_ids = inputs
        offsets = time_ids[None, None, :] - starts[:, None, None] - frame_ids[None, :, None] * HOP
        valid = (offsets >= 0) & (offsets < WIN)
        clipped = jnp.clip(offsets, 0, WIN - 1)
        cosine, sine_part = wave_values(clipped, band_ids[:, None, None], tapers_in[:, None, None])
        kernel = jnp.stack([cosine, sine_part], axis=1)
        kernel = jnp.where(valid[:, None], kernel, 0.0).astype(jnp.bfloat16)
        kernel = kernel.reshape(per_group * 2 * FR, samples)
        return lax.dot_general(
            kernel, trace_rows, (((1,), (1,)), ((), ())), preferred_element_type=jnp.float32
        )

    group_count = NB // per_group
    grouped = lax.map(
        one_group,
        (
            band_start.reshape(group_count, per_group),
            taper_len.reshape(group_count, per_group),
            jnp.arange(NB, dtype=jnp.int32).reshape(group_count, per_group),
        ),
    )
    return grouped.reshape(NB, 2, FR, row_total)


def coherence(s_ii, s_ix, s_xx):
    return ((s_ii - s_xx) ** 2 + 4.0 * s_ix**2) / (s_ii + s_xx + epsilon) ** 2


def column_work(conc_block, band_weight):
    xl_cols = conc_block.shape[3]
    row_count = conc_block.shape[2]
    extended = with_halo(conc_block, (("band", 3),), RAD_XL + 1)
    field_f32 = extended.astype(jnp.float32)
    rows_pad = jnp.pad(field_f32, ((0, 0), (0, 0), (1, 1), (0, 0)))
    grad_in = 0.5 * (rows_pad[:, :, 2:, 1:-1] - rows_pad[:, :, :-2, 1:-1])
    grad_xl = 0.5 * (field_f32[..., 2:] - field_f32[..., :-2])
    col_count = grad_xl.shape[3]
    global_cols = lax.axis_index("band") * xl_cols - RAD_XL + jnp.arange(col_count, dtype=jnp.int32)
    inside = ((global_cols >= 0) & (global_cols < xl_cols * lax.axis_size("band"))).astype(
        jnp.float32
    )
    grad_in = grad_in * inside
    grad_xl = grad_xl * inside
    smoothed = []
    for product in (grad_in * grad_in, grad_in * grad_xl, grad_xl * grad_xl):
        inl_pad = jnp.pad(product, ((0, 0), (0, 0), (RAD_INL, RAD_INL), (0, 0)))
        inline_sum = inl_pad[:, :, 0:row_count]
        for offset in range(1, 2 * RAD_INL + 1):
            inline_sum = inline_sum + inl_pad[:, :, offset : offset + row_count]
        summed = inline_sum[..., 0:xl_cols]
        for offset in range(1, 2 * RAD_XL + 1):
            summed = summed + inline_sum[..., offset : offset + xl_cols]
        smoothed.append(summed)
    scores = band_weight[:, None, None, None] * (
        1.0 - coherence(smoothed[0], smoothed[1], smoothed[2])
    )
    return jnp.sum(scores, axis=0)


def on_device(traces, band_start, taper_len, band_weight, labels):
    il_rows, xl_cols, samples = traces.shape
    trace_rows = traces.reshape(il_rows * xl_cols, samples).astype(jnp.bfloat16)
    coeffs = band_coeffs(trace_rows, band_start, taper_len)
    coeffs = coeffs.reshape(NB, 2, FR, il_rows, xl_cols)
    band_power = coeffs[:, 0] ** 2 + coeffs[:, 1] ** 2
    amplitude = jnp.log(1.0 + band_power)
    average = jnp.mean(amplitude, axis=0, keepdims=True)
    concentration = (amplitude / (1.0 + average)).astype(jnp.bfloat16)
    spread = lax.all_to_all(concentration, ("inl", "xl"), split_axis=1, concat_axis=2, tiled=True)
    partial_cols = column_work(spread, band_weight)
    by_slab = lax.all_to_all(partial_cols, ("inl", "xl"), split_axis=1, concat_axis=0, tiled=True)
    fault_map = lax.all_to_all(by_slab, "band", split_axis=0, concat_axis=2, tiled=True)
    misfit = (jnp.tanh(fault_map) - labels.astype(jnp.float32)[None]) ** 2
    return (fault_map, misfit)


MESH = pl.DeviceIdType.MESH
EDGE = 16
PAD = 8
CHUNK = 512
HALO = RAD_XL + 1


def wave_block(first, start, taper, rows):
    lane = lax.broadcasted_iota(jnp.int32, (rows, 2 * NB), 1)
    time = lax.broadcasted_iota(jnp.int32, (rows, 2 * NB), 0) + first
    late = (lane >= NB).astype(jnp.int32)
    band = lane - late * NB
    lag = time - (start & 127) - late * HOP
    valid = (lag >= 0) & (lag < WIN)
    lag_f = lag.astype(jnp.float32)
    tapers = jnp.minimum(
        jnp.minimum(lag_f + 1.0, WIN - lag_f) / (taper.astype(jnp.float32) + 1.0), 1.0
    )
    tapers = jnp.where(valid, tapers, 0.0)
    cycles = ((band + 1) * lag) & (WIN - 1)
    quarter = (cycles + 32) >> 6
    x = (cycles - quarter * 64).astype(jnp.float32) * (2.0 * math.pi / WIN)
    z = x * x
    sin_x = x + x * z * (-1.6666654611e-1 + z * (8.3321608736e-3 + z * -1.9515295891e-4))
    cos_x = (1.0 - 0.5 * z) + z * z * (
        4.166664568298827e-2 + z * (-1.388731625493765e-3 + z * 2.443315711809948e-5)
    )
    swap = (quarter & 1) == 1
    cos_sign = jnp.where(((quarter + 1) & 2) == 2, -tapers, tapers)
    sin_sign = jnp.where((quarter & 2) == 2, -tapers, tapers)
    cosine = cos_sign * jnp.where(swap, sin_x, cos_x)
    sine = sin_sign * jnp.where(swap, cos_x, sin_x)
    return cosine.astype(jnp.bfloat16), sine.astype(jnp.bfloat16)


def split_bf16(x):
    high = x.astype(jnp.bfloat16)
    return high, (x - high.astype(jnp.float32)).astype(jnp.bfloat16)


def dot32(a, b):
    return jnp.dot(a, b, preferred_element_type=jnp.float32)


def twice(x):
    return jnp.concatenate([x, x], axis=1)


def fused_kernel(
    slabs, n_band, traces, start_ref, taper_ref, weight_ref, fault_ref,
    t32, tb, start_at, taper_at, weight_at,
    waves, power, field, packed, halo, corner, prods, part_out, part_in,
    load_sem, small_sem, main_send, main_recv, left_send, left_recv, right_send, right_recv,
    cross_send, cross_recv, cross_left_send, cross_left_recv, cross_right_send,
    cross_right_recv, part_send, part_recv,
):
    group = lax.axis_index("groups")
    beta = lax.axis_index("band")
    n_xl = lax.axis_size("xl")
    inl = lax.axis_index("inl")
    core = lax.axis_index("xl")
    slab = inl * n_xl + core
    il_rows, xl_cols = traces.shape[0], traces.shape[1]
    rows = il_rows * xl_cols

    def device(band_at, slab_at):
        return (group, band_at, slab_at // n_xl, slab_at % n_xl)

    smalls = [
        pltpu.make_async_copy(source, to, small_sem.at[i])
        for i, (source, to) in enumerate(
            (
                (start_ref, start_at),
                (taper_ref, taper_at),
                (weight_ref, weight_at),
            )
        )
    ]
    for small in smalls:
        small.start()
    loads = [
        pltpu.make_async_copy(
            traces.at[:, :, pl.ds(i * CHUNK, CHUNK)],
            t32.at[:, :, pl.ds(i * CHUNK, CHUNK)],
            load_sem.at[i],
        )
        for i in range(traces.shape[2] // CHUNK)
    ]
    for load in loads:
        load.start()

    barrier = pltpu.get_barrier_semaphore()
    for db in range(n_band):
        for ds in range(slabs):
            if db or ds:
                pl.semaphore_signal(
                    barrier,
                    inc=1,
                    device_id=device((beta + db) % n_band, (slab + ds) % slabs),
                    device_id_type=MESH,
                )

    for small in smalls:
        small.wait()
    start = twice(start_at[...])
    taper = twice(taper_at[...])
    for first in range(0, 512, 64):
        cosine, sine = wave_block(first, start, taper, 64)
        waves[first : first + 64, 0 : 2 * NB] = cosine
        waves[first : first + 64, 2 * NB : 4 * NB] = sine

    field[0:2, 3 + 9 * inl] = jnp.zeros((2,) + field.shape[2:], field.dtype)
    @pl.when(beta == 0)
    def _():
        halo[:, :, 0] = jnp.zeros((2, n_xl) + halo.shape[3:], halo.dtype)
        corner[:, 0] = jnp.zeros((2,) + corner.shape[2:], corner.dtype)

    @pl.when(beta == n_band - 1)
    def _():
        halo[:, :, 1] = jnp.zeros((2, n_xl) + halo.shape[3:], halo.dtype)
        corner[:, 1] = jnp.zeros((2,) + corner.shape[2:], corner.dtype)

    for row in range(2):
        prods[:, :, 2 + row + 10 * inl] = jnp.zeros((2, 3) + prods.shape[3:], jnp.float32)

    samples = traces.shape[2]
    tb[:, samples:] = jnp.zeros((rows, 128), jnp.bfloat16)

    def land(chunk):
        loads[chunk].wait()
        span = slice(chunk * CHUNK, (chunk + 1) * CHUNK)
        tb[:, span] = t32[:, :, span].reshape(rows, CHUNK).astype(jnp.bfloat16)

    def one_step(step):
        if step % 4 == 1 and step < 13:
            land(step // 4 + 1)
        at = step * 128
        coeffs = dot32(tb[:, pl.ds(at, 512)], waves[...])
        cosine, sine = coeffs[:, 0 : 2 * NB], coeffs[:, 2 * NB :]
        power[step] = cosine * cosine + sine * sine

    land(0)

    first_step = start >> 7
    half_r = lax.broadcasted_iota(jnp.int32, (2 * NB, 2 * NB), 0) // NB
    half_c = lax.broadcasted_iota(jnp.int32, (2 * NB, 2 * NB), 1) // NB
    mean_mat = jnp.where(half_r == half_c, 1.0 / NB, 0.0).astype(jnp.bfloat16)

    def concentrations(m, slot):
        for j in range(2):
            pair = m * 2 + j
            chosen = power[pair]
            for q in range(1, 7):
                chosen = jnp.where(first_step == q, power[pair + q], chosen)
            amplitude = jnp.log(1.0 + chosen)
            high, low = split_bf16(amplitude)
            average = dot32(high, mean_mat) + dot32(low, mean_mat)
            value = (amplitude / (1.0 + average)).astype(jnp.bfloat16)
            field[slot, mine, middle, j * 2 * NB : (j + 1) * 2 * NB] = value.reshape(
                il_rows, xl_cols, 2 * NB
            )

    mine = pl.ds(4 + core * il_rows, il_rows)
    border_from = pl.ds(4 + core * il_rows + 1 - inl, 3)
    border_to = pl.ds(1 + 11 * inl, 3)
    at_border = core == 1 - inl
    middle = pl.ds(EDGE, xl_cols)
    first_cols, last_cols = pl.ds(EDGE, EDGE), pl.ds(xl_cols, EDGE)
    left_band, right_band = (beta + n_band - 1) % n_band, (beta + 1) % n_band
    has_left, has_right = beta > 0, beta < n_band - 1

    def place_of(m):
        owner, half = m % 2, m // 2
        return owner, half, half + 2 * ((core + owner) % 2)

    def one_hot(ones):
        return jnp.where(ones, 1.0, 0.0).astype(jnp.bfloat16)

    out_at = lax.broadcasted_iota(jnp.int32, (96, 8 * EDGE), 0)
    in_at = lax.broadcasted_iota(jnp.int32, (96, 8 * EDGE), 1)
    from_right = in_at // (4 * EDGE)
    in_row = in_at % (4 * EDGE) // EDGE
    in_col = in_at % EDGE - from_right * (EDGE - HALO)
    in_code = jnp.where(
        (in_col >= 0) & (in_col < HALO), from_right * 64 + in_row * HALO + in_col, -2
    )
    corner_code = jnp.where(
        out_at % 16 < 3 * HALO, out_at // 16 % 2 * 64 + out_at % 16 + (1 - inl) * HALO, -1
    )
    out_code = jnp.where(out_at < 64, out_at // 32 * 64 + out_at % 32, corner_code)
    pack_mat = one_hot(in_code == out_code)

    def unpack_matrix(depth, first):
        to = lax.broadcasted_iota(jnp.int32, (8 * EDGE, 2 * depth), 0)
        at = lax.broadcasted_iota(jnp.int32, (8 * EDGE, 2 * depth), 1)
        to_right = to // (4 * EDGE)
        col = to % EDGE - (1 - to_right) * (EDGE - HALO)
        code = (to % (4 * EDGE) // EDGE - first) * HALO + col
        return one_hot(
            (col >= 0) & (col < HALO) & (code == at % depth) & (to_right == at // depth)
        )

    unpack_mat = unpack_matrix(32, 0)
    unpack_corner = unpack_matrix(16, inl)

    def pack(m):
        _, _, slot = place_of(m)
        edges = jnp.concatenate(
            [
                field[slot, mine, first_cols].reshape(4 * EDGE, 4 * NB),
                field[slot, mine, last_cols].reshape(4 * EDGE, 4 * NB),
            ],
            axis=0,
        )
        packed[m] = dot32(pack_mat, edges).astype(jnp.bfloat16)

    def unpack(half, block, halves, matrix):
        edges = dot32(matrix, halves).astype(jnp.bfloat16)
        to = pl.ds(4 * block, 4)
        field[half, to, 0:EDGE] = edges[: 4 * EDGE].reshape(4, EDGE, 4 * NB)
        field[half, to, EDGE + xl_cols :] = edges[4 * EDGE :].reshape(4, EDGE, 4 * NB)

    sent = []

    def send(asked, source, to, send_sem, recv_sem, band_at, slab_at):
        copy = pltpu.make_async_remote_copy(
            src_ref=source,
            dst_ref=to,
            send_sem=send_sem,
            recv_sem=recv_sem,
            device_id=device(band_at, slab_at),
            device_id_type=MESH,
        )
        sent.append((asked, copy))

        @pl.when(asked)
        def _():
            copy.start()

    def send_rows(m):
        owner, half, slot = place_of(m)
        own_chip, other_chip = inl * n_xl + owner, (1 - inl) * n_xl + owner
        send(at_border, field.at[slot, border_from, middle], field.at[half, border_to, middle],
             cross_send.at[m], cross_recv.at[half], beta, other_chip)
        send(core == 1 - owner, field.at[slot, mine, middle], field.at[half, mine, middle],
             main_send.at[m], main_recv.at[half], beta, own_chip)

    def send_edges(m):
        owner, half, _ = place_of(m)
        own_chip, other_chip = inl * n_xl + owner, (1 - inl) * n_xl + owner
        send(at_border & has_left, packed.at[m, pl.ds(64, 16)], corner.at[half, 1],
             cross_left_send.at[m], cross_left_recv.at[half], left_band, other_chip)
        send(at_border & has_right, packed.at[m, pl.ds(80, 16)], corner.at[half, 0],
             cross_right_send.at[m], cross_right_recv.at[half], right_band, other_chip)
        send(has_left, packed.at[m, pl.ds(0, 32)], halo.at[half, core, 1],
             left_send.at[m], left_recv.at[half * 2 + core], left_band, own_chip)
        send(has_right, packed.at[m, pl.ds(32, 32)], halo.at[half, core, 0],
             right_send.at[m], right_recv.at[half * 2 + core], right_band, own_chip)

    for step in range(8):
        one_step(step)
    for m in range(4):
        if m:
            pack(m - 1)
        for step in range(8 + 2 * m, min(10 + 2 * m, 14)):
            one_step(step)
        concentrations(m, place_of(m)[2])
        if m:
            send_edges(m - 1)
        else:
            pl.semaphore_wait(barrier, n_band * slabs - 1)
        send_rows(m)
    pack(3)
    send_edges(3)

    wide = xl_cols + 2 * PAD
    cells = pl.ds(EDGE - PAD, wide)
    shape = (wide, xl_cols + 2 * EDGE)
    out_x = lax.broadcasted_iota(jnp.int32, shape, 0) + (EDGE - PAD)
    in_x = lax.broadcasted_iota(jnp.int32, shape, 1)
    diff_mat = (
        (in_x == out_x + 1).astype(jnp.float32) - (in_x == out_x - 1).astype(jnp.float32)
    ).astype(jnp.bfloat16)
    out_x = lax.broadcasted_iota(jnp.int32, (xl_cols, wide), 0)
    in_x = lax.broadcasted_iota(jnp.int32, (xl_cols, wide), 1) - PAD
    at_x = in_x + beta * xl_cols
    near = (jnp.abs(in_x - out_x) <= RAD_XL) & (at_x >= 0) & (at_x < xl_cols * n_band)
    box_mat = near.astype(jnp.float32).astype(jnp.bfloat16)
    box_twice = twice(box_mat)
    weights = twice(twice(weight_at[...]))
    row = lax.broadcasted_iota(jnp.int32, (16, 4 * NB), 0)
    lane = lax.broadcasted_iota(jnp.int32, (16, 4 * NB), 1)
    w_high, w_low = split_bf16(weights)
    w_high = w_high.astype(jnp.float32)
    w_low = w_low.astype(jnp.float32)
    weight_mat = jnp.where(
        row == lane // NB, w_high, jnp.where(row - 4 == lane // NB, w_low, 0.0)
    ).astype(jnp.bfloat16)

    def landed(block, sem):
        pltpu.make_async_remote_copy(
            src_ref=block,
            dst_ref=block,
            send_sem=main_send.at[0],
            recv_sem=sem,
            device_id=device(beta, inl * n_xl + 1 - core),
            device_id_type=MESH,
        ).wait_recv()

    def own_chip_landed(half):
        landed(
            field.at[half, pl.ds(4 + (1 - core) * il_rows, il_rows), middle], main_recv.at[half]
        )

        @pl.when(has_right)
        def _():
            for source in range(2):
                landed(halo.at[half, source, 1], left_recv.at[half * 2 + source])

        @pl.when(has_left)
        def _():
            for source in range(2):
                landed(halo.at[half, source, 0], right_recv.at[half * 2 + source])

        for source in range(2):
            halves = jnp.concatenate([halo[half, source, 0], halo[half, source, 1]], axis=0)
            unpack(half, 1 + source, halves, unpack_mat)

    def other_chip_landed(half):
        landed(field.at[half, pl.ds(12 - 11 * inl, 3), middle], cross_recv.at[half])

        @pl.when(has_right)
        def _():
            landed(corner.at[half, 1], cross_left_recv.at[half])

        @pl.when(has_left)
        def _():
            landed(corner.at[half, 0], cross_right_recv.at[half])

        halves = jnp.concatenate([corner[half, 0], corner[half, 1]], axis=0)
        unpack(half, 3 - 3 * inl, halves, unpack_corner)

    def one_product(half, turn):
        i = 4 + turn + inl * (7 - 2 * turn)
        grad_xl = dot32(diff_mat, field[half, i])
        grad_in = field[half, i + 1, cells].astype(jnp.float32) - field[
            half, i - 1, cells
        ].astype(jnp.float32)
        prods[half, 0, i] = grad_in * grad_in
        prods[half, 1, i] = grad_in * grad_xl
        prods[half, 2, i] = grad_xl * grad_xl

    parts = []

    def slab_scores(half, turn):
        place = turn + inl * (1 - 2 * turn)
        base = 2 + place * il_rows
        slot = turn * 2 + half
        sums = [[] for _ in range(il_rows)]
        for which in range(3):
            p = [prods[half, which, base + r] for r in range(8)]
            a, b, c = p[1] + p[2], p[5] + p[6], p[3] + p[4]
            ac, bc = a + c, b + c
            for r, total in enumerate((p[0] + ac, p[5] + ac, p[2] + bc, p[7] + bc)):
                high, low = split_bf16(total)
                sums[r].append(dot32(box_twice, jnp.concatenate([high, low], axis=0)))
        scores = []
        for s_ii, s_ix, s_xx in sums:
            total = s_ii + s_xx + 4.0 * epsilon
            gap = s_ii - s_xx
            scores.append(1.0 - (gap * gap + 4.0 * (s_ix * s_ix)) / (total * total))
        high, low = split_bf16(jnp.concatenate(scores, axis=0))
        nt = (((1,), (1,)), ((), ()))
        both = lax.dot_general(
            weight_mat, high, nt, preferred_element_type=jnp.float32
        ) + lax.dot_general(weight_mat, low, nt, preferred_element_type=jnp.float32)
        both = both[0:8]
        both = both + pltpu.roll(both, 4, 0)
        upper = lax.broadcasted_iota(jnp.int32, (8, 128), 0) < 4
        part_out[slot] = jnp.where(upper, both[:, 0:128], both[:, 128:256])
        part = pltpu.make_async_remote_copy(
            src_ref=part_out.at[slot],
            dst_ref=part_in.at[beta],
            send_sem=part_send.at[slot],
            recv_sem=part_recv.at[beta],
            device_id=device(half * 2 + core, inl * n_xl + place),
            device_id_type=MESH,
        )
        own = (half * 2 + core == beta) & (place == core)
        parts.append((part, own))

        @pl.when(own)
        def _():
            part_in[beta] = part_out[slot]

        @pl.when(jnp.logical_not(own))
        def _():
            part.start()

    for half in range(2):
        own_chip_landed(half)
        for turn in range(7):
            one_product(half, turn)
        slab_scores(half, 0)
        other_chip_landed(half)
        for turn in range(7, 10):
            one_product(half, turn)
        slab_scores(half, 1)

    for source in range(n_band):
        @pl.when(jnp.logical_not((beta % 2 == core) & (beta == source)))
        def _(source=source):
            pltpu.make_async_remote_copy(
                src_ref=part_out.at[0],
                dst_ref=part_in.at[source],
                send_sem=part_send.at[0],
                recv_sem=part_recv.at[source],
                device_id=device((beta + 1) % n_band, slab),
                device_id_type=MESH,
            ).wait_recv()

    for source in range(n_band):
        fault_ref[source] = part_in[source]

    for asked, copy in sent:
        @pl.when(asked)
        def _(copy=copy):
            copy.wait_send()

    for part, own in parts:
        @pl.when(jnp.logical_not(own))
        def _(part=part):
            part.wait_send()


def final_kernel(parts_ref, labels_ref, fault_ref, misfit_ref):
    first_half = lax.broadcasted_iota(jnp.int32, (8, 128), 1) < 64
    labels = labels_ref[...].astype(jnp.float32)
    halves = [[], []]
    for c in range(0, parts_ref.shape[0], 2):
        one, two = parts_ref[c], parts_ref[c + 1]
        halves[0].append(jnp.where(first_half, one, pltpu.roll(two, 64, 1)))
        halves[1].append(jnp.where(first_half, pltpu.roll(one, 64, 1), two))
    frames = fault_ref.shape[0]
    for odd in range(2):
        blocks = jnp.concatenate(halves[odd], axis=1)
        for two in range(2):
            i = two * 2 + odd
            here = blocks[two * 4 : two * 4 + 4]
            miss = jnp.tanh(here) - labels[i : i + 1]
            miss = miss * miss
            for f in range(frames):
                fault_ref[f, i : i + 1] = here[f : f + 1]
                misfit_ref[f, i : i + 1] = miss[f : f + 1]


def fused(traces, band_start, taper_len, band_weight, labels):
    il_rows, xl_cols, samples = traces.shape
    rows = il_rows * xl_cols
    n_band = lax.axis_size("band")
    slabs = lax.axis_size("inl") * lax.axis_size("xl")
    frames = FR // n_band
    out = jax.ShapeDtypeStruct((frames, il_rows, xl_cols * n_band), jnp.float32)
    vmem = pl.BlockSpec(memory_space=pltpu.VMEM)
    dma = pltpu.SemaphoreType.DMA
    parts = pl.pallas_call(
        functools.partial(fused_kernel, slabs, n_band),
        out_shape=jax.ShapeDtypeStruct((n_band, 8, 128), jnp.float32),
        in_specs=[pl.BlockSpec(memory_space=pltpu.HBM)] * 4,
        out_specs=vmem,
        scratch_shapes=[
            pltpu.VMEM((il_rows, xl_cols, samples), jnp.float32),
            pltpu.VMEM((rows, samples + 128), jnp.bfloat16),
            pltpu.VMEM((1, NB), jnp.int32),
            pltpu.VMEM((1, NB), jnp.int32),
            pltpu.VMEM((1, NB), jnp.float32),
            pltpu.VMEM((512, 4 * NB), jnp.bfloat16),
            pltpu.VMEM((14, rows, 2 * NB), jnp.float32),
            pltpu.VMEM((4, 16, xl_cols + 2 * EDGE, 4 * NB), jnp.bfloat16),
            pltpu.VMEM((4, 96, 4 * NB), jnp.bfloat16),
            pltpu.VMEM((2, 2, 2, 32, 4 * NB), jnp.bfloat16),
            pltpu.VMEM((2, 2, 16, 4 * NB), jnp.bfloat16),
            pltpu.VMEM((2, 3, 16, xl_cols + 2 * PAD, 4 * NB), jnp.float32),
            pltpu.VMEM((slabs, 8, 128), jnp.float32),
            pltpu.VMEM((n_band, 8, 128), jnp.float32),
            dma((samples // CHUNK,)),
            dma((3,)),
            dma((4,)),
            dma((2,)),
            dma((4,)),
            dma((4,)),
            dma((4,)),
            dma((4,)),
            dma((4,)),
            dma((2,)),
            dma((4,)),
            dma((2,)),
            dma((4,)),
            dma((2,)),
            dma((slabs,)),
            dma((n_band,)),
        ],
        compiler_params=pltpu.CompilerParams(
            collective_id=0, has_side_effects=True, vmem_limit_bytes=32 * 1024 * 1024
        ),
    )(
        *[
            pltpu.with_memory_space_constraint(operand, pltpu.HBM)
            for operand in (
                traces,
                band_start.reshape(1, NB),
                taper_len.reshape(1, NB),
                band_weight.reshape(1, NB),
            )
        ]
    )
    return pl.pallas_call(
        final_kernel, out_shape=(out, out), in_specs=[vmem, vmem], out_specs=(vmem, vmem)
    )(
        pltpu.with_memory_space_constraint(parts, pltpu.VMEM),
        pltpu.with_memory_space_constraint(labels, pltpu.VMEM),
    )


def solution(mesh):
    shape = mesh.shape
    square = shape["band"] == 4 and shape["inl"] == 2 and shape["xl"] == 2
    return jax.shard_map(
        fused if square else on_device,
        mesh=mesh,
        in_specs=(
            P(("groups", "inl", "xl"), "band", None),
            P(),
            P(),
            P(),
            P(("groups", "inl", "xl"), None),
        ),
        out_specs=(
            P(("groups", "band"), ("inl", "xl"), None),
            P(("groups", "band"), ("inl", "xl"), None),
        ),
        check_vma=False,
    )
```

```python
import functools
import math

import jax
import jax.numpy as jnp
from jax import lax
from jax.experimental import pallas as pl
from jax.experimental.pallas import tpu as pltpu
from jax.sharding import PartitionSpec as P

WIN = 256
HOP = 64
FR = 16
NB = 64
RAD_INL = 2
RAD_XL = 4


epsilon = 1e-06


def with_halo(cells, sides, width):
    for axis, dim in sides:
        count = lax.axis_size(axis)
        ends = count - 1
        head = lax.slice_in_dim(cells, 0, width, axis=dim)
        tail = lax.slice_in_dim(cells, cells.shape[dim] - width, cells.shape[dim], axis=dim)
        cells = jnp.concatenate(
            [
                lax.ppermute(tail, axis, [(i, (i + 1) % count) for i in range(ends)]),
                cells,
                lax.ppermute(head, axis, [((i + 1) % count, i) for i in range(ends)]),
            ],
            axis=dim,
        )
    return cells


def wave_values(offsets, band_ids, taper_lens):
    shifted = offsets.astype(jnp.float32)
    ramp_len = taper_lens.astype(jnp.float32) + 1.0
    tapers = jnp.minimum(jnp.minimum((shifted + 1.0) / ramp_len, (WIN - shifted) / ramp_len), 1.0)
    cycles = (band_ids + 1) * offsets % WIN
    angles = cycles.astype(jnp.float32) * (2.0 * math.pi / WIN)
    return (tapers * jnp.cos(angles), tapers * jnp.sin(angles))


def band_coeffs(trace_rows, band_start, taper_len):
    row_total = trace_rows.shape[0]
    samples = trace_rows.shape[1]
    per_group = 8
    time_ids = jnp.arange(samples, dtype=jnp.int32)
    frame_ids = jnp.arange(FR, dtype=jnp.int32)

    def one_group(inputs):
        starts, tapers_in, band_ids = inputs
        offsets = time_ids[None, None, :] - starts[:, None, None] - frame_ids[None, :, None] * HOP
        valid = (offsets >= 0) & (offsets < WIN)
        clipped = jnp.clip(offsets, 0, WIN - 1)
        cosine, sine_part = wave_values(clipped, band_ids[:, None, None], tapers_in[:, None, None])
        kernel = jnp.stack([cosine, sine_part], axis=1)
        kernel = jnp.where(valid[:, None], kernel, 0.0).astype(jnp.bfloat16)
        kernel = kernel.reshape(per_group * 2 * FR, samples)
        return lax.dot_general(
            kernel, trace_rows, (((1,), (1,)), ((), ())), preferred_element_type=jnp.float32
        )

    group_count = NB // per_group
    grouped = lax.map(
        one_group,
        (
            band_start.reshape(group_count, per_group),
            taper_len.reshape(group_count, per_group),
            jnp.arange(NB, dtype=jnp.int32).reshape(group_count, per_group),
        ),
    )
    return grouped.reshape(NB, 2, FR, row_total)


def coherence(s_ii, s_ix, s_xx):
    return ((s_ii - s_xx) ** 2 + 4.0 * s_ix**2) / (s_ii + s_xx + epsilon) ** 2


def column_work(conc_block, band_weight):
    xl_cols = conc_block.shape[3]
    row_count = conc_block.shape[2]
    extended = with_halo(conc_block, (("band", 3),), RAD_XL + 1)
    field_f32 = extended.astype(jnp.float32)
    rows_pad = jnp.pad(field_f32, ((0, 0), (0, 0), (1, 1), (0, 0)))
    grad_in = 0.5 * (rows_pad[:, :, 2:, 1:-1] - rows_pad[:, :, :-2, 1:-1])
    grad_xl = 0.5 * (field_f32[..., 2:] - field_f32[..., :-2])
    col_count = grad_xl.shape[3]
    global_cols = lax.axis_index("band") * xl_cols - RAD_XL + jnp.arange(col_count, dtype=jnp.int32)
    inside = ((global_cols >= 0) & (global_cols < xl_cols * lax.axis_size("band"))).astype(
        jnp.float32
    )
    grad_in = grad_in * inside
    grad_xl = grad_xl * inside
    smoothed = []
    for product in (grad_in * grad_in, grad_in * grad_xl, grad_xl * grad_xl):
        inl_pad = jnp.pad(product, ((0, 0), (0, 0), (RAD_INL, RAD_INL), (0, 0)))
        inline_sum = inl_pad[:, :, 0:row_count]
        for offset in range(1, 2 * RAD_INL + 1):
            inline_sum = inline_sum + inl_pad[:, :, offset : offset + row_count]
        summed = inline_sum[..., 0:xl_cols]
        for offset in range(1, 2 * RAD_XL + 1):
            summed = summed + inline_sum[..., offset : offset + xl_cols]
        smoothed.append(summed)
    scores = band_weight[:, None, None, None] * (
        1.0 - coherence(smoothed[0], smoothed[1], smoothed[2])
    )
    return jnp.sum(scores, axis=0)


def on_device(traces, band_start, taper_len, band_weight, labels):
    il_rows, xl_cols, samples = traces.shape
    trace_rows = traces.reshape(il_rows * xl_cols, samples).astype(jnp.bfloat16)
    coeffs = band_coeffs(trace_rows, band_start, taper_len)
    coeffs = coeffs.reshape(NB, 2, FR, il_rows, xl_cols)
    band_power = coeffs[:, 0] ** 2 + coeffs[:, 1] ** 2
    amplitude = jnp.log(1.0 + band_power)
    average = jnp.mean(amplitude, axis=0, keepdims=True)
    concentration = (amplitude / (1.0 + average)).astype(jnp.bfloat16)
    spread = lax.all_to_all(concentration, ("inl", "xl"), split_axis=1, concat_axis=2, tiled=True)
    partial_cols = column_work(spread, band_weight)
    by_slab = lax.all_to_all(partial_cols, ("inl", "xl"), split_axis=1, concat_axis=0, tiled=True)
    fault_map = lax.all_to_all(by_slab, "band", split_axis=0, concat_axis=2, tiled=True)
    misfit = (jnp.tanh(fault_map) - labels.astype(jnp.float32)[None]) ** 2
    return (fault_map, misfit)


MESH = pl.DeviceIdType.MESH
EDGE = 16
CHUNK = 512
HALO = RAD_XL + 1


def wave_block(first, start, taper, rows):
    lane = lax.broadcasted_iota(jnp.int32, (rows, 2 * NB), 1)
    late = (lane >= NB).astype(jnp.int32)
    time = lax.broadcasted_iota(jnp.int32, (rows, 2 * NB), 0) + first
    band = lane - late * NB
    lag = time - (start & 127) + late * HOP
    valid = (lag >= 0) & (lag < WIN)
    lag_f = lag.astype(jnp.float32)
    tapers = jnp.minimum(
        jnp.minimum(lag_f + 1.0, WIN - lag_f) / (taper.astype(jnp.float32) + 1.0), 1.0
    )
    tapers = jnp.where(valid, tapers, 0.0)
    cycles = ((band + 1) * lag) & (WIN - 1)
    quarter = (cycles + 32) >> 6
    x = (cycles - quarter * 64).astype(jnp.float32) * (2.0 * math.pi / WIN)
    z = x * x
    sin_x = x + x * z * (-1.6666654611e-1 + z * (8.3321608736e-3 + z * -1.9515295891e-4))
    cos_x = (1.0 - 0.5 * z) + z * z * (
        4.166664568298827e-2 + z * (-1.388731625493765e-3 + z * 2.443315711809948e-5)
    )
    swap = (quarter & 1) == 1
    cos_sign = jnp.where(((quarter + 1) & 2) == 2, -tapers, tapers)
    sin_sign = jnp.where((quarter & 2) == 2, -tapers, tapers)
    cosine = cos_sign * jnp.where(swap, sin_x, cos_x)
    sine = sin_sign * jnp.where(swap, cos_x, sin_x)
    return cosine, sine


def split_bf16(x):
    high = x.astype(jnp.bfloat16)
    return high, (x - high.astype(jnp.float32)).astype(jnp.bfloat16)


def dot32(a, b):
    return jnp.dot(a, b, preferred_element_type=jnp.float32)


def twice(x):
    return jnp.concatenate([x, x], axis=1)


def fused_kernel(
    slabs, n_band, traces, start_ref, taper_ref, weight_ref, fault_ref,
    t32, tb, start_at, taper_at, weight_at,
    waves, power, field, packed, halo, corner, prods_0, prods_1, part_out, part_in,
    load_sem, small_sem, main_send, main_recv, left_send, left_recv, right_send, right_recv,
    cross_send, cross_recv, cross_left_send, cross_left_recv, cross_right_send,
    cross_right_recv, part_send, part_recv,
):
    group = lax.axis_index("groups")
    beta = lax.axis_index("band")
    n_xl = lax.axis_size("xl")
    inl = lax.axis_index("inl")
    core = lax.axis_index("xl")
    slab = inl * n_xl + core
    il_rows, xl_cols = traces.shape[0], traces.shape[1]
    rows = il_rows * xl_cols

    def device(band_at, slab_at):
        return (group, band_at, slab_at // n_xl, slab_at % n_xl)

    smalls = [
        pltpu.make_async_copy(source, to, small_sem.at[i])
        for i, (source, to) in enumerate(
            (
                (start_ref, start_at),
                (taper_ref, taper_at),
                (weight_ref, weight_at),
            )
        )
    ]
    for small in smalls:
        small.start()
    loads = [
        pltpu.make_async_copy(
            traces.at[:, :, pl.ds(i * CHUNK, CHUNK)],
            t32.at[:, :, pl.ds(i * CHUNK, CHUNK)],
            load_sem.at[i],
        )
        for i in range(traces.shape[2] // CHUNK)
    ]
    for load in loads:
        load.start()

    barrier = pltpu.get_barrier_semaphore()
    for db in range(n_band):
        for ds in range(slabs):
            if db or ds:
                pl.semaphore_signal(
                    barrier,
                    inc=1,
                    device_id=device((beta + db) % n_band, (slab + ds) % slabs),
                    device_id_type=MESH,
                )

    field[0:2, 3 + 9 * inl] = jnp.zeros((2,) + field.shape[2:], field.dtype)
    @pl.when(beta == 0)
    def _():
        halo[:, :, 0] = jnp.zeros((2, n_xl) + halo.shape[3:], halo.dtype)
        corner[:, 0] = jnp.zeros((2,) + corner.shape[2:], corner.dtype)

    @pl.when(beta == n_band - 1)
    def _():
        halo[:, :, 1] = jnp.zeros((2, n_xl) + halo.shape[3:], halo.dtype)
        corner[:, 1] = jnp.zeros((2,) + corner.shape[2:], corner.dtype)

    prods = (prods_0, prods_1)
    for half in range(2):
        for row in range(2):
            prods[half][:, 2 + row + 10 * inl] = jnp.zeros((3,) + prods_0.shape[2:], jnp.float32)

    half_r = lax.broadcasted_iota(jnp.int32, (2 * NB, 2 * NB), 0) // NB
    half_c = lax.broadcasted_iota(jnp.int32, (2 * NB, 2 * NB), 1) // NB
    mean_mat = jnp.where(half_r == half_c, 1.0 / NB, 0.0).astype(jnp.bfloat16)

    mean_mat = jnp.concatenate([mean_mat, mean_mat], axis=0)
    def one_hot(ones):
        return jnp.where(ones, 1.0, 0.0).astype(jnp.bfloat16)

    out_at = lax.broadcasted_iota(jnp.int32, (96, 8 * EDGE), 0)
    in_at = lax.broadcasted_iota(jnp.int32, (96, 8 * EDGE), 1)
    from_right = in_at // (4 * EDGE)
    in_row = in_at % (4 * EDGE) // EDGE
    in_col = in_at % EDGE - from_right * (EDGE - HALO)
    in_code = jnp.where(
        (in_col >= 0) & (in_col < HALO), from_right * 64 + in_row * HALO + in_col, -2
    )
    corner_code = jnp.where(
        out_at % 16 < 3 * HALO, out_at // 16 % 2 * 64 + out_at % 16 + (1 - inl) * HALO, -1
    )
    out_code = jnp.where(out_at < 64, out_at // 32 * 64 + out_at % 32, corner_code)
    pack_mat = one_hot(in_code == out_code)

    def column_of(place):
        near = jnp.where(place < xl_cols + RAD_XL, place - xl_cols - RAD_XL, place - RAD_XL)
        far = jnp.where(
            place < xl_cols + 2 * RAD_XL + 2,
            jnp.where(place == xl_cols + 2 * RAD_XL, -HALO, xl_cols + RAD_XL),
            4 * xl_cols,
        )
        return jnp.where(
            place < xl_cols, place, jnp.where(place < xl_cols + 2 * RAD_XL, near, far)
        )

    def unpack_matrix(depth, first):
        to = lax.broadcasted_iota(jnp.int32, (4 * EDGE, 2 * depth), 0)
        at = lax.broadcasted_iota(jnp.int32, (4 * EDGE, 2 * depth), 1)
        column = column_of(xl_cols + to % EDGE)
        row = to // EDGE - first
        west = (at < depth) & (column < 0) & (at == row * HALO + column + HALO)
        east = (at >= depth) & (column < 2 * xl_cols) & (
            at - depth == row * HALO + column - xl_cols
        )
        fits = (row >= 0) & (row < 4)
        return one_hot(fits & (west | ((column >= xl_cols) & east)))

    unpack_mat = unpack_matrix(32, 0)
    unpack_corner = unpack_matrix(16, inl)

    wide = xl_cols + 2 * RAD_XL
    cells = pl.ds(0, wide)
    shape = (wide, xl_cols + EDGE)
    out_x = column_of(lax.broadcasted_iota(jnp.int32, shape, 0))
    in_x = column_of(lax.broadcasted_iota(jnp.int32, shape, 1))
    diff_mat = (
        (in_x == out_x + 1).astype(jnp.float32) - (in_x == out_x - 1).astype(jnp.float32)
    ).astype(jnp.bfloat16)
    out_x = lax.broadcasted_iota(jnp.int32, (xl_cols, wide), 0)
    in_x = column_of(lax.broadcasted_iota(jnp.int32, (xl_cols, wide), 1))
    at_x = in_x + beta * xl_cols
    near = (jnp.abs(in_x - out_x) <= RAD_XL) & (at_x >= 0) & (at_x < xl_cols * n_band)
    box_mat = near.astype(jnp.float32)
    box_mats = [box_mat.astype(jnp.bfloat16), (2.0 * box_mat).astype(jnp.bfloat16)]
    for small in smalls:
        small.wait()
    start = twice(start_at[...])
    taper = twice(taper_at[...])
    early = lax.broadcasted_iota(jnp.int32, (HOP, 2 * NB), 1) < NB
    last = [jnp.zeros((HOP, 2 * NB), jnp.float32)] * 2
    for first in range(0, 512, 2 * HOP):
        now = wave_block(first, start, taper, HOP)
        for i in range(2):
            lanes = slice(i * 2 * NB, (i + 1) * 2 * NB)
            waves[first : first + HOP, lanes] = jnp.where(early, now[i], last[i]).astype(
                jnp.bfloat16
            )
            waves[first + HOP : first + 2 * HOP, lanes] = pltpu.roll(now[i], NB, 1).astype(
                jnp.bfloat16
            )
        last = now
    samples = traces.shape[2]
    tb[:, samples:] = jnp.zeros((rows, 128), jnp.bfloat16)

    def land(chunk):
        loads[chunk].wait()
        span = slice(chunk * CHUNK, (chunk + 1) * CHUNK)
        tb[:, span] = t32[:, :, span].reshape(rows, CHUNK).astype(jnp.bfloat16)

    def one_step(step):
        if step % 4 == 1 and step < 13:
            land(step // 4 + 1)
        at = step * 128
        coeffs = dot32(tb[:, pl.ds(at, 512)], waves[...])
        cosine, sine = coeffs[:, 0 : 2 * NB], coeffs[:, 2 * NB :]
        power[step] = cosine * cosine + sine * sine

    land(0)

    first_step = start >> 7
    def concentrations(m, slot):
        for j in range(2):
            pair = m * 2 + j
            chosen = power[pair]
            for q in range(1, 7):
                chosen = jnp.where(first_step == q, power[pair + q], chosen)
            amplitude = jnp.log(1.0 + chosen)
            average = dot32(jnp.concatenate(split_bf16(amplitude), axis=1), mean_mat)
            value = (amplitude / (1.0 + average)).astype(jnp.bfloat16)
            field[slot, mine, middle, j * 2 * NB : (j + 1) * 2 * NB] = value.reshape(
                il_rows, xl_cols, 2 * NB
            )

    mine = pl.ds(4 + core * il_rows, il_rows)
    border_from = pl.ds(4 + core * il_rows + 1 - inl, 3)
    border_to = pl.ds(1 + 11 * inl, 3)
    at_border = core == 1 - inl
    middle = pl.ds(0, xl_cols)
    first_cols, last_cols = pl.ds(0, EDGE), pl.ds(xl_cols - EDGE, EDGE)
    left_band, right_band = (beta + n_band - 1) % n_band, (beta + 1) % n_band
    has_left, has_right = beta > 0, beta < n_band - 1

    def place_of(m):
        owner, half = m % 2, m // 2
        return owner, half, half + 2 * ((core + owner) % 2)

    def pack(m):
        _, _, slot = place_of(m)
        edges = jnp.concatenate(
            [
                field[slot, mine, first_cols].reshape(4 * EDGE, 4 * NB),
                field[slot, mine, last_cols].reshape(4 * EDGE, 4 * NB),
            ],
            axis=0,
        )
        packed[m] = dot32(pack_mat, edges).astype(jnp.bfloat16)

    def unpack(half, block, halves, matrix):
        edges = dot32(matrix, halves).astype(jnp.bfloat16)
        field[half, pl.ds(4 * block, 4), pl.ds(xl_cols, EDGE)] = edges.reshape(4, EDGE, 4 * NB)

    sent = []
    prompt = (beta > 0) | (inl > 0)
    patient = jnp.logical_not(prompt)

    def send(asked, source, to, send_sem, recv_sem, band_at, slab_at):
        copy = pltpu.make_async_remote_copy(
            src_ref=source,
            dst_ref=to,
            send_sem=send_sem,
            recv_sem=recv_sem,
            device_id=device(band_at, slab_at),
            device_id_type=MESH,
        )
        sent.append((asked, copy))

        @pl.when(asked & prompt)
        def _():
            copy.start()

    def send_rows(m):
        owner, half, slot = place_of(m)
        own_chip, other_chip = inl * n_xl + owner, (1 - inl) * n_xl + owner
        send(at_border, field.at[slot, border_from, middle], field.at[half, border_to, middle],
             cross_send.at[m], cross_recv.at[half], beta, other_chip)
        send(core == 1 - owner, field.at[slot, mine, middle], field.at[half, mine, middle],
             main_send.at[m], main_recv.at[half], beta, own_chip)

    def send_edges(m):
        owner, half, _ = place_of(m)
        own_chip, other_chip = inl * n_xl + owner, (1 - inl) * n_xl + owner
        send(at_border & has_left, packed.at[m, pl.ds(64, 16)], corner.at[half, 1],
             cross_left_send.at[m], cross_left_recv.at[half], left_band, other_chip)
        send(at_border & has_right, packed.at[m, pl.ds(80, 16)], corner.at[half, 0],
             cross_right_send.at[m], cross_right_recv.at[half], right_band, other_chip)
        send(has_left, packed.at[m, pl.ds(0, 32)], halo.at[half, core, 1],
             left_send.at[m], left_recv.at[half * 2 + core], left_band, own_chip)
        send(has_right, packed.at[m, pl.ds(32, 32)], halo.at[half, core, 0],
             right_send.at[m], right_recv.at[half * 2 + core], right_band, own_chip)

    for step in range(8):
        one_step(step)
    for m in range(4):
        for step in (range(0), range(8, 12), range(12, 14), range(0))[m]:
            one_step(step)
        concentrations(m, place_of(m)[2])
        if m == 0:
            @pl.when(prompt)
            def _():
                pl.semaphore_wait(barrier, n_band * slabs - 1)

        send_rows(m)
        pack(m)
        send_edges(m)

    @pl.when(patient)
    def _():
        pl.semaphore_wait(barrier, n_band * slabs - 1)
        for asked, copy in sent:
            @pl.when(asked)
            def _(copy=copy):
                copy.start()


    weights = twice(twice(weight_at[...]))
    row = lax.broadcasted_iota(jnp.int32, (16, 4 * NB), 0)
    lane = lax.broadcasted_iota(jnp.int32, (16, 4 * NB), 1)
    w_high, w_low = split_bf16(weights)
    w_high = w_high.astype(jnp.float32)
    w_low = w_low.astype(jnp.float32)
    weight_mat = jnp.where(
        row == lane // NB, w_high, jnp.where(row - 4 == lane // NB, w_low, 0.0)
    ).astype(jnp.bfloat16)

    def landed(block, sem):
        pltpu.make_async_remote_copy(
            src_ref=block,
            dst_ref=block,
            send_sem=main_send.at[0],
            recv_sem=sem,
            device_id=device(beta, inl * n_xl + 1 - core),
            device_id_type=MESH,
        ).wait_recv()

    def own_chip_landed(half):
        landed(
            field.at[half, pl.ds(4 + (1 - core) * il_rows, il_rows), middle], main_recv.at[half]
        )

        @pl.when(has_right)
        def _():
            for source in range(2):
                landed(halo.at[half, source, 1], left_recv.at[half * 2 + source])

        @pl.when(has_left)
        def _():
            for source in range(2):
                landed(halo.at[half, source, 0], right_recv.at[half * 2 + source])

        for source in range(2):
            halves = jnp.concatenate([halo[half, source, 0], halo[half, source, 1]], axis=0)
            unpack(half, 1 + source, halves, unpack_mat)

    def other_chip_landed(half):
        landed(field.at[half, pl.ds(12 - 11 * inl, 3), middle], cross_recv.at[half])

        @pl.when(has_right)
        def _():
            landed(corner.at[half, 1], cross_left_recv.at[half])

        @pl.when(has_left)
        def _():
            landed(corner.at[half, 0], cross_right_recv.at[half])

        halves = jnp.concatenate([corner[half, 0], corner[half, 1]], axis=0)
        unpack(half, 3 - 3 * inl, halves, unpack_corner)

    def one_product(half, turn):
        i = 4 + turn + inl * (7 - 2 * turn)
        grad_xl = dot32(diff_mat, field[half, i])
        grad_in = field[half, i + 1, cells].astype(jnp.float32) - field[
            half, i - 1, cells
        ].astype(jnp.float32)
        prods[half][0, i] = grad_in * grad_in
        prods[half][1, i] = grad_in * grad_xl
        prods[half][2, i] = grad_xl * grad_xl

    parts = []

    def slab_scores(half, turn):
        place = turn + inl * (1 - 2 * turn)
        base = 2 + place * il_rows
        slot = turn * 2 + half
        highs, lows = [], []
        for lanes in (slice(0, 128), slice(128, 256)):
            sums = [[] for _ in range(il_rows)]
            for which in range(3):
                p = [prods[half][which, base + r, :, lanes] for r in range(8)]
                a, b, c = p[1] + p[2], p[5] + p[6], p[3] + p[4]
                ac, bc = a + c, b + c
                box = box_mats[which == 1]
                for r, total in enumerate((p[0] + ac, p[5] + ac, p[2] + bc, p[7] + bc)):
                    high, low = split_bf16(total)
                    sums[r].append(dot32(box, high) + dot32(box, low))
            scores = []
            for s_ii, s_ix, s_xx in sums:
                total = s_ii + s_xx + 4.0 * epsilon
                gap = s_ii - s_xx
                scores.append(1.0 - (gap * gap + s_ix * s_ix) / (total * total))
            high, low = split_bf16(jnp.concatenate(scores, axis=0))
            highs.append(high)
            lows.append(low)
        high, low = jnp.concatenate(highs, axis=1), jnp.concatenate(lows, axis=1)
        nt = (((1,), (1,)), ((), ()))
        both = lax.dot_general(
            weight_mat, high, nt, preferred_element_type=jnp.float32
        ) + lax.dot_general(weight_mat, low, nt, preferred_element_type=jnp.float32)
        both = both[0:8]
        both = both + pltpu.roll(both, 4, 0)
        upper = lax.broadcasted_iota(jnp.int32, (8, 128), 0) < 4
        part_out[slot] = jnp.where(upper, both[:, 0:128], both[:, 128:256])
        part = pltpu.make_async_remote_copy(
            src_ref=part_out.at[slot],
            dst_ref=part_in.at[beta],
            send_sem=part_send.at[slot],
            recv_sem=part_recv.at[beta],
            device_id=device(half * 2 + core, inl * n_xl + place),
            device_id_type=MESH,
        )
        own = (half * 2 + core == beta) & (place == core)
        parts.append((part, own))

        @pl.when(own)
        def _():
            part_in[beta] = part_out[slot]

        @pl.when(jnp.logical_not(own))
        def _():
            part.start()

    for half in range(2):
        own_chip_landed(half)
        for turn in range(7):
            one_product(half, turn)
        slab_scores(half, 0)
        other_chip_landed(half)
        for turn in range(7, 10):
            one_product(half, turn)
        slab_scores(half, 1)

    for source in range(n_band):
        @pl.when(jnp.logical_not((beta % 2 == core) & (beta == source)))
        def _(source=source):
            pltpu.make_async_remote_copy(
                src_ref=part_out.at[0],
                dst_ref=part_in.at[source],
                send_sem=part_send.at[0],
                recv_sem=part_recv.at[source],
                device_id=device((beta + 1) % n_band, slab),
                device_id_type=MESH,
            ).wait_recv()

    for source in range(n_band):
        fault_ref[source] = part_in[source]

    for asked, copy in sent:
        @pl.when(asked)
        def _(copy=copy):
            copy.wait_send()

    for part, own in parts:
        @pl.when(jnp.logical_not(own))
        def _(part=part):
            part.wait_send()


def final_kernel(parts_ref, labels_ref, fault_ref, misfit_ref):
    first_half = lax.broadcasted_iota(jnp.int32, (8, 128), 1) < 64
    labels = labels_ref[...].astype(jnp.float32)
    halves = [[], []]
    for c in range(0, parts_ref.shape[0], 2):
        one, two = parts_ref[c], parts_ref[c + 1]
        halves[0].append(jnp.where(first_half, one, pltpu.roll(two, 64, 1)))
        halves[1].append(jnp.where(first_half, pltpu.roll(one, 64, 1), two))
    frames = fault_ref.shape[0]
    for odd in range(2):
        blocks = jnp.concatenate(halves[odd], axis=1)
        for two in range(2):
            i = two * 2 + odd
            here = blocks[two * 4 : two * 4 + 4]
            miss = jnp.tanh(here) - labels[i : i + 1]
            miss = miss * miss
            for f in range(frames):
                fault_ref[f, i : i + 1] = here[f : f + 1]
                misfit_ref[f, i : i + 1] = miss[f : f + 1]


def fused(traces, band_start, taper_len, band_weight, labels):
    il_rows, xl_cols, samples = traces.shape
    rows = il_rows * xl_cols
    n_band = lax.axis_size("band")
    slabs = lax.axis_size("inl") * lax.axis_size("xl")
    frames = FR // n_band
    out = jax.ShapeDtypeStruct((frames, il_rows, xl_cols * n_band), jnp.float32)
    vmem = pl.BlockSpec(memory_space=pltpu.VMEM)
    dma = pltpu.SemaphoreType.DMA
    parts = pl.pallas_call(
        functools.partial(fused_kernel, slabs, n_band),
        out_shape=jax.ShapeDtypeStruct((n_band, 8, 128), jnp.float32),
        in_specs=[pl.BlockSpec(memory_space=pltpu.HBM)] * 4,
        out_specs=vmem,
        scratch_shapes=[
            pltpu.VMEM((il_rows, xl_cols, samples), jnp.float32),
            pltpu.VMEM((rows, samples + 128), jnp.bfloat16),
            pltpu.VMEM((1, NB), jnp.int32),
            pltpu.VMEM((1, NB), jnp.int32),
            pltpu.VMEM((1, NB), jnp.float32),
            pltpu.VMEM((512, 4 * NB), jnp.bfloat16),
            pltpu.VMEM((14, rows, 2 * NB), jnp.float32),
            pltpu.VMEM((4, 16, xl_cols + EDGE, 4 * NB), jnp.bfloat16),
            pltpu.VMEM((4, 96, 4 * NB), jnp.bfloat16),
            pltpu.VMEM((2, 2, 2, 32, 4 * NB), jnp.bfloat16),
            pltpu.VMEM((2, 2, 16, 4 * NB), jnp.bfloat16),
            pltpu.VMEM((3, 16, xl_cols + 2 * RAD_XL, 4 * NB), jnp.float32),
            pltpu.VMEM((3, 16, xl_cols + 2 * RAD_XL, 4 * NB), jnp.float32),
            pltpu.VMEM((slabs, 8, 128), jnp.float32),
            pltpu.VMEM((n_band, 8, 128), jnp.float32),
            dma((samples // CHUNK,)),
            dma((3,)),
            dma((4,)),
            dma((2,)),
            dma((4,)),
            dma((4,)),
            dma((4,)),
            dma((4,)),
            dma((4,)),
            dma((2,)),
            dma((4,)),
            dma((2,)),
            dma((4,)),
            dma((2,)),
            dma((slabs,)),
            dma((n_band,)),
        ],
        compiler_params=pltpu.CompilerParams(
            collective_id=0, has_side_effects=True, vmem_limit_bytes=32 * 1024 * 1024
        ),
    )(
        *[
            pltpu.with_memory_space_constraint(operand, pltpu.HBM)
            for operand in (
                traces,
                band_start.reshape(1, NB),
                taper_len.reshape(1, NB),
                band_weight.reshape(1, NB),
            )
        ]
    )
    return pl.pallas_call(
        final_kernel, out_shape=(out, out), in_specs=[vmem, vmem], out_specs=(vmem, vmem)
    )(
        pltpu.with_memory_space_constraint(parts, pltpu.VMEM),
        pltpu.with_memory_space_constraint(labels, pltpu.VMEM),
    )


def solution(mesh):
    shape = mesh.shape
    square = shape["band"] == 4 and shape["inl"] == 2 and shape["xl"] == 2
    return jax.shard_map(
        fused if square else on_device,
        mesh=mesh,
        in_specs=(
            P(("groups", "inl", "xl"), "band", None),
            P(),
            P(),
            P(),
            P(("groups", "inl", "xl"), None),
        ),
        out_specs=(
            P(("groups", "band"), ("inl", "xl"), None),
            P(("groups", "band"), ("inl", "xl"), None),
        ),
        check_vma=False,
    )
```

```python
import functools
import math

import jax
import jax.numpy as jnp
from jax import lax
from jax.experimental import pallas as pl
from jax.experimental.pallas import tpu as pltpu
from jax.sharding import PartitionSpec as P

WIN = 256
HOP = 64
FR = 16
NB = 64
RAD_INL = 2
RAD_XL = 4


epsilon = 1e-06


def with_halo(cells, sides, width):
    for axis, dim in sides:
        count = lax.axis_size(axis)
        ends = count - 1
        head = lax.slice_in_dim(cells, 0, width, axis=dim)
        tail = lax.slice_in_dim(cells, cells.shape[dim] - width, cells.shape[dim], axis=dim)
        cells = jnp.concatenate(
            [
                lax.ppermute(tail, axis, [(i, (i + 1) % count) for i in range(ends)]),
                cells,
                lax.ppermute(head, axis, [((i + 1) % count, i) for i in range(ends)]),
            ],
            axis=dim,
        )
    return cells


def wave_values(offsets, band_ids, taper_lens):
    shifted = offsets.astype(jnp.float32)
    ramp_len = taper_lens.astype(jnp.float32) + 1.0
    tapers = jnp.minimum(jnp.minimum((shifted + 1.0) / ramp_len, (WIN - shifted) / ramp_len), 1.0)
    cycles = (band_ids + 1) * offsets % WIN
    angles = cycles.astype(jnp.float32) * (2.0 * math.pi / WIN)
    return (tapers * jnp.cos(angles), tapers * jnp.sin(angles))


def band_coeffs(trace_rows, band_start, taper_len):
    row_total = trace_rows.shape[0]
    samples = trace_rows.shape[1]
    per_group = 8
    time_ids = jnp.arange(samples, dtype=jnp.int32)
    frame_ids = jnp.arange(FR, dtype=jnp.int32)

    def one_group(inputs):
        starts, tapers_in, band_ids = inputs
        offsets = time_ids[None, None, :] - starts[:, None, None] - frame_ids[None, :, None] * HOP
        valid = (offsets >= 0) & (offsets < WIN)
        clipped = jnp.clip(offsets, 0, WIN - 1)
        cosine, sine_part = wave_values(clipped, band_ids[:, None, None], tapers_in[:, None, None])
        kernel = jnp.stack([cosine, sine_part], axis=1)
        kernel = jnp.where(valid[:, None], kernel, 0.0).astype(jnp.bfloat16)
        kernel = kernel.reshape(per_group * 2 * FR, samples)
        return lax.dot_general(
            kernel, trace_rows, (((1,), (1,)), ((), ())), preferred_element_type=jnp.float32
        )

    group_count = NB // per_group
    grouped = lax.map(
        one_group,
        (
            band_start.reshape(group_count, per_group),
            taper_len.reshape(group_count, per_group),
            jnp.arange(NB, dtype=jnp.int32).reshape(group_count, per_group),
        ),
    )
    return grouped.reshape(NB, 2, FR, row_total)


def coherence(s_ii, s_ix, s_xx):
    return ((s_ii - s_xx) ** 2 + 4.0 * s_ix**2) / (s_ii + s_xx + epsilon) ** 2


def column_work(conc_block, band_weight):
    xl_cols = conc_block.shape[3]
    row_count = conc_block.shape[2]
    extended = with_halo(conc_block, (("band", 3),), RAD_XL + 1)
    field_f32 = extended.astype(jnp.float32)
    rows_pad = jnp.pad(field_f32, ((0, 0), (0, 0), (1, 1), (0, 0)))
    grad_in = 0.5 * (rows_pad[:, :, 2:, 1:-1] - rows_pad[:, :, :-2, 1:-1])
    grad_xl = 0.5 * (field_f32[..., 2:] - field_f32[..., :-2])
    col_count = grad_xl.shape[3]
    global_cols = lax.axis_index("band") * xl_cols - RAD_XL + jnp.arange(col_count, dtype=jnp.int32)
    inside = ((global_cols >= 0) & (global_cols < xl_cols * lax.axis_size("band"))).astype(
        jnp.float32
    )
    grad_in = grad_in * inside
    grad_xl = grad_xl * inside
    smoothed = []
    for product in (grad_in * grad_in, grad_in * grad_xl, grad_xl * grad_xl):
        inl_pad = jnp.pad(product, ((0, 0), (0, 0), (RAD_INL, RAD_INL), (0, 0)))
        inline_sum = inl_pad[:, :, 0:row_count]
        for offset in range(1, 2 * RAD_INL + 1):
            inline_sum = inline_sum + inl_pad[:, :, offset : offset + row_count]
        summed = inline_sum[..., 0:xl_cols]
        for offset in range(1, 2 * RAD_XL + 1):
            summed = summed + inline_sum[..., offset : offset + xl_cols]
        smoothed.append(summed)
    scores = band_weight[:, None, None, None] * (
        1.0 - coherence(smoothed[0], smoothed[1], smoothed[2])
    )
    return jnp.sum(scores, axis=0)


def on_device(traces, band_start, taper_len, band_weight, labels):
    il_rows, xl_cols, samples = traces.shape
    trace_rows = traces.reshape(il_rows * xl_cols, samples).astype(jnp.bfloat16)
    coeffs = band_coeffs(trace_rows, band_start, taper_len)
    coeffs = coeffs.reshape(NB, 2, FR, il_rows, xl_cols)
    band_power = coeffs[:, 0] ** 2 + coeffs[:, 1] ** 2
    amplitude = jnp.log(1.0 + band_power)
    average = jnp.mean(amplitude, axis=0, keepdims=True)
    concentration = (amplitude / (1.0 + average)).astype(jnp.bfloat16)
    spread = lax.all_to_all(concentration, ("inl", "xl"), split_axis=1, concat_axis=2, tiled=True)
    partial_cols = column_work(spread, band_weight)
    by_slab = lax.all_to_all(partial_cols, ("inl", "xl"), split_axis=1, concat_axis=0, tiled=True)
    fault_map = lax.all_to_all(by_slab, "band", split_axis=0, concat_axis=2, tiled=True)
    misfit = (jnp.tanh(fault_map) - labels.astype(jnp.float32)[None]) ** 2
    return (fault_map, misfit)


MESH = pl.DeviceIdType.MESH
EDGE = 16
CHUNK = 512
HALO = RAD_XL + 1


def wave_block(first, start, taper, rows):
    lane = lax.broadcasted_iota(jnp.int32, (rows, 2 * NB), 1)
    late = (lane >= NB).astype(jnp.int32)
    time = lax.broadcasted_iota(jnp.int32, (rows, 2 * NB), 0) + first
    band = lane - late * NB
    lag = time - (start & 127) + late * HOP
    valid = (lag >= 0) & (lag < WIN)
    lag_f = lag.astype(jnp.float32)
    tapers = jnp.minimum(
        jnp.minimum(lag_f + 1.0, WIN - lag_f) / (taper.astype(jnp.float32) + 1.0), 1.0
    )
    tapers = jnp.where(valid, tapers, 0.0)
    cycles = ((band + 1) * lag) & (WIN - 1)
    quarter = (cycles + 32) >> 6
    x = (cycles - quarter * 64).astype(jnp.float32) * (2.0 * math.pi / WIN)
    z = x * x
    sin_x = x + x * z * (-1.6666654611e-1 + z * (8.3321608736e-3 + z * -1.9515295891e-4))
    cos_x = (1.0 - 0.5 * z) + z * z * (
        4.166664568298827e-2 + z * (-1.388731625493765e-3 + z * 2.443315711809948e-5)
    )
    swap = (quarter & 1) == 1
    cos_sign = jnp.where(((quarter + 1) & 2) == 2, -tapers, tapers)
    sin_sign = jnp.where((quarter & 2) == 2, -tapers, tapers)
    cosine = cos_sign * jnp.where(swap, sin_x, cos_x)
    sine = sin_sign * jnp.where(swap, cos_x, sin_x)
    return cosine, sine


def split_bf16(x):
    high = x.astype(jnp.bfloat16)
    return high, (x - high.astype(jnp.float32)).astype(jnp.bfloat16)


def dot32(a, b):
    return jnp.dot(a, b, preferred_element_type=jnp.float32)


def twice(x):
    return jnp.concatenate([x, x], axis=1)


def fused_kernel(
    slabs, n_band, traces, start_ref, taper_ref, weight_ref, fault_ref,
    t32, tb, start_at, taper_at, weight_at,
    waves, power, field, packed, halo, corner, prods_0, prods_1, part_out, part_in,
    load_sem, small_sem, main_send, main_recv, left_send, left_recv, right_send, right_recv,
    cross_send, cross_recv, cross_left_send, cross_left_recv, cross_right_send,
    cross_right_recv, part_send, part_recv, far_in,
):
    group = lax.axis_index("groups")
    beta = lax.axis_index("band")
    n_xl = lax.axis_size("xl")
    inl = lax.axis_index("inl")
    core = lax.axis_index("xl")
    slab = inl * n_xl + core
    il_rows, xl_cols = traces.shape[0], traces.shape[1]
    rows = il_rows * xl_cols

    def device(band_at, slab_at):
        return (group, band_at, slab_at // n_xl, slab_at % n_xl)

    smalls = [
        pltpu.make_async_copy(source, to, small_sem.at[i])
        for i, (source, to) in enumerate(
            (
                (start_ref, start_at),
                (taper_ref, taper_at),
                (weight_ref, weight_at),
            )
        )
    ]
    for small in smalls:
        small.start()
    loads = [
        pltpu.make_async_copy(
            traces.at[:, :, pl.ds(i * CHUNK, CHUNK)],
            t32.at[:, :, pl.ds(i * CHUNK, CHUNK)],
            load_sem.at[i],
        )
        for i in range(traces.shape[2] // CHUNK)
    ]
    for load in loads:
        load.start()

    barrier = pltpu.get_barrier_semaphore()
    for to_band in range(n_band):
        for ds in range(slabs):
            @pl.when((to_band >= beta - 1) & ((to_band != beta) | (ds > 0)))
            def _(to_band=to_band, ds=ds):
                pl.semaphore_signal(
                    barrier,
                    inc=1,
                    device_id=device(to_band, (slab + ds) % slabs),
                    device_id_type=MESH,
                )

    entered = jnp.minimum(beta + 2, n_band) * slabs - 1

    field[0:2, 3 + 9 * inl] = jnp.zeros((2,) + field.shape[2:], field.dtype)
    @pl.when(beta == 0)
    def _():
        halo[:, :, 0] = jnp.zeros((2, n_xl) + halo.shape[3:], halo.dtype)
        corner[:, 0] = jnp.zeros((2,) + corner.shape[2:], corner.dtype)

    @pl.when(beta == n_band - 1)
    def _():
        halo[:, :, 1] = jnp.zeros((2, n_xl) + halo.shape[3:], halo.dtype)
        corner[:, 1] = jnp.zeros((2,) + corner.shape[2:], corner.dtype)

    prods = (prods_0, prods_1)
    for half in range(2):
        for row in range(2):
            prods[half][:, 2 + row + 10 * inl] = jnp.zeros((3,) + prods_0.shape[2:], jnp.float32)

    half_r = lax.broadcasted_iota(jnp.int32, (2 * NB, 2 * NB), 0) // NB
    half_c = lax.broadcasted_iota(jnp.int32, (2 * NB, 2 * NB), 1) // NB
    mean_mat = jnp.where(half_r == half_c, 1.0 / NB, 0.0).astype(jnp.bfloat16)

    mean_mat = jnp.concatenate([mean_mat, mean_mat], axis=0)
    def one_hot(ones):
        return jnp.where(ones, 1.0, 0.0).astype(jnp.bfloat16)

    out_at = lax.broadcasted_iota(jnp.int32, (96, 8 * EDGE), 0)
    in_at = lax.broadcasted_iota(jnp.int32, (96, 8 * EDGE), 1)
    from_right = in_at // (4 * EDGE)
    in_row = in_at % (4 * EDGE) // EDGE
    in_col = in_at % EDGE - from_right * (EDGE - HALO)
    in_code = jnp.where(
        (in_col >= 0) & (in_col < HALO), from_right * 64 + in_row * HALO + in_col, -2
    )
    corner_code = jnp.where(
        out_at % 16 < 3 * HALO, out_at // 16 % 2 * 64 + out_at % 16 + (1 - inl) * HALO, -1
    )
    out_code = jnp.where(out_at < 64, out_at // 32 * 64 + out_at % 32, corner_code)
    pack_mat = one_hot(in_code == out_code)

    def column_of(place):
        near = jnp.where(place < xl_cols + RAD_XL, place - xl_cols - RAD_XL, place - RAD_XL)
        far = jnp.where(
            place < xl_cols + 2 * RAD_XL + 2,
            jnp.where(place == xl_cols + 2 * RAD_XL, -HALO, xl_cols + RAD_XL),
            4 * xl_cols,
        )
        return jnp.where(
            place < xl_cols, place, jnp.where(place < xl_cols + 2 * RAD_XL, near, far)
        )

    def unpack_matrix(depth, first):
        to = lax.broadcasted_iota(jnp.int32, (4 * EDGE, 2 * depth), 0)
        at = lax.broadcasted_iota(jnp.int32, (4 * EDGE, 2 * depth), 1)
        column = column_of(xl_cols + to % EDGE)
        row = to // EDGE - first
        west = (at < depth) & (column < 0) & (at == row * HALO + column + HALO)
        east = (at >= depth) & (column < 2 * xl_cols) & (
            at - depth == row * HALO + column - xl_cols
        )
        fits = (row >= 0) & (row < 4)
        return one_hot(fits & (west | ((column >= xl_cols) & east)))

    unpack_mat = unpack_matrix(32, 0)
    unpack_corner = unpack_matrix(16, inl)

    wide = xl_cols + 2 * RAD_XL
    cells = pl.ds(0, wide)
    shape = (wide, xl_cols + EDGE)
    out_x = column_of(lax.broadcasted_iota(jnp.int32, shape, 0))
    in_x = column_of(lax.broadcasted_iota(jnp.int32, shape, 1))
    diff_mat = (
        (in_x == out_x + 1).astype(jnp.float32) - (in_x == out_x - 1).astype(jnp.float32)
    ).astype(jnp.bfloat16)
    out_x = lax.broadcasted_iota(jnp.int32, (xl_cols, wide), 0)
    in_x = column_of(lax.broadcasted_iota(jnp.int32, (xl_cols, wide), 1))
    at_x = in_x + beta * xl_cols
    near = (jnp.abs(in_x - out_x) <= RAD_XL) & (at_x >= 0) & (at_x < xl_cols * n_band)
    box_mat = near.astype(jnp.float32)
    box_mats = [box_mat.astype(jnp.bfloat16), (2.0 * box_mat).astype(jnp.bfloat16)]
    for small in smalls:
        small.wait()
    start = twice(start_at[...])
    taper = twice(taper_at[...])
    early = lax.broadcasted_iota(jnp.int32, (HOP, 2 * NB), 1) < NB
    last = [jnp.zeros((HOP, 2 * NB), jnp.float32)] * 2
    for first in range(0, 512, 2 * HOP):
        now = wave_block(first, start, taper, HOP)
        for i in range(2):
            lanes = slice(i * 2 * NB, (i + 1) * 2 * NB)
            waves[first : first + HOP, lanes] = jnp.where(early, now[i], last[i]).astype(
                jnp.bfloat16
            )
            waves[first + HOP : first + 2 * HOP, lanes] = pltpu.roll(now[i], NB, 1).astype(
                jnp.bfloat16
            )
        last = now
    samples = traces.shape[2]
    tb[:, samples:] = jnp.zeros((rows, 128), jnp.bfloat16)

    def land(chunk):
        loads[chunk].wait()
        span = slice(chunk * CHUNK, (chunk + 1) * CHUNK)
        tb[:, span] = t32[:, :, span].reshape(rows, CHUNK).astype(jnp.bfloat16)

    def one_step(step):
        if step % 4 == 1 and step < 13:
            land(step // 4 + 1)
        at = step * 128
        coeffs = dot32(tb[:, pl.ds(at, 512)], waves[...])
        cosine, sine = coeffs[:, 0 : 2 * NB], coeffs[:, 2 * NB :]
        power[step] = cosine * cosine + sine * sine

    land(0)

    first_step = start >> 7
    def concentrations(m, slot):
        for j in range(2):
            pair = m * 2 + j
            chosen = power[pair]
            for q in range(1, 7):
                chosen = jnp.where(first_step == q, power[pair + q], chosen)
            amplitude = jnp.log(1.0 + chosen)
            average = dot32(jnp.concatenate(split_bf16(amplitude), axis=1), mean_mat)
            value = (amplitude / (1.0 + average)).astype(jnp.bfloat16)
            field[slot, mine, middle, j * 2 * NB : (j + 1) * 2 * NB] = value.reshape(
                il_rows, xl_cols, 2 * NB
            )

    mine = pl.ds(4 + core * il_rows, il_rows)
    border_from = pl.ds(4 + core * il_rows + 1 - inl, 3)
    border_to = pl.ds(1 + 11 * inl, 3)
    at_border = core == 1 - inl
    middle = pl.ds(0, xl_cols)
    first_cols, last_cols = pl.ds(0, EDGE), pl.ds(xl_cols - EDGE, EDGE)
    left_band, right_band = (beta + n_band - 1) % n_band, (beta + 1) % n_band
    has_left, has_right = beta > 0, beta < n_band - 1

    def place_of(m):
        owner, half = m % 2, m // 2
        return owner, half, half + 2 * ((core + owner) % 2)

    def pack(m):
        _, _, slot = place_of(m)
        edges = jnp.concatenate(
            [
                field[slot, mine, first_cols].reshape(4 * EDGE, 4 * NB),
                field[slot, mine, last_cols].reshape(4 * EDGE, 4 * NB),
            ],
            axis=0,
        )
        packed[m] = dot32(pack_mat, edges).astype(jnp.bfloat16)

    def unpack(half, block, halves, matrix):
        edges = dot32(matrix, halves).astype(jnp.bfloat16)
        field[half, pl.ds(4 * block, 4), pl.ds(xl_cols, EDGE)] = edges.reshape(4, EDGE, 4 * NB)

    sent = []

    def send(asked, source, to, send_sem, recv_sem, band_at, slab_at):
        copy = pltpu.make_async_remote_copy(
            src_ref=source,
            dst_ref=to,
            send_sem=send_sem,
            recv_sem=recv_sem,
            device_id=device(band_at, slab_at),
            device_id_type=MESH,
        )
        sent.append((asked, copy))

        @pl.when(asked)
        def _():
            copy.start()

    def send_all(m):
        owner, half, slot = place_of(m)
        own_chip, other_chip = inl * n_xl + owner, (1 - inl) * n_xl + owner
        send(at_border, field.at[slot, border_from, middle], field.at[half, border_to, middle],
             cross_send.at[m], cross_recv.at[half], beta, other_chip)
        send(core == 1 - owner, field.at[slot, mine, middle], field.at[half, mine, middle],
             main_send.at[m], main_recv.at[half], beta, own_chip)
        send(has_left, packed.at[m, pl.ds(0, 32)], halo.at[half, core, 1],
             left_send.at[m], left_recv.at[half * 2 + core], left_band, own_chip)
        send(has_right, packed.at[m, pl.ds(32, 32)], halo.at[half, core, 0],
             right_send.at[m], right_recv.at[half * 2 + core], right_band, own_chip)
        send(at_border & has_left, packed.at[m, pl.ds(64, 16)], corner.at[half, 1],
             cross_left_send.at[m], cross_left_recv.at[half], left_band, other_chip)
        send(at_border & has_right, packed.at[m, pl.ds(80, 16)], corner.at[half, 0],
             cross_right_send.at[m], cross_right_recv.at[half], right_band, other_chip)

    for step in range(8):
        one_step(step)
    for m in range(4):
        for step in (range(0), range(8, 12), range(12, 14), range(0))[m]:
            one_step(step)
        concentrations(m, place_of(m)[2])
        if m == 0:
            pl.semaphore_wait(barrier, entered)

            for to_band in range(n_band - 2):
                @pl.when(beta >= to_band + 2)
                def _(to_band=to_band):
                    for to_core in range(2):
                        pl.semaphore_signal(
                            far_in,
                            inc=1,
                            device_id=device(to_band, inl * n_xl + to_core),
                            device_id_type=MESH,
                        )

        pack(m)
        send_all(m)

    weights = twice(twice(weight_at[...]))
    row = lax.broadcasted_iota(jnp.int32, (16, 4 * NB), 0)
    lane = lax.broadcasted_iota(jnp.int32, (16, 4 * NB), 1)
    w_high, w_low = split_bf16(weights)
    w_high = w_high.astype(jnp.float32)
    w_low = w_low.astype(jnp.float32)
    weight_mat = jnp.where(
        row == lane // NB, w_high, jnp.where(row - 4 == lane // NB, w_low, 0.0)
    ).astype(jnp.bfloat16)

    def landed(block, sem):
        pltpu.make_async_remote_copy(
            src_ref=block,
            dst_ref=block,
            send_sem=main_send.at[0],
            recv_sem=sem,
            device_id=device(beta, inl * n_xl + 1 - core),
            device_id_type=MESH,
        ).wait_recv()

    def own_chip_landed(half):
        landed(
            field.at[half, pl.ds(4 + (1 - core) * il_rows, il_rows), middle], main_recv.at[half]
        )

        @pl.when(has_right)
        def _():
            for source in range(2):
                landed(halo.at[half, source, 1], left_recv.at[half * 2 + source])

        @pl.when(has_left)
        def _():
            for source in range(2):
                landed(halo.at[half, source, 0], right_recv.at[half * 2 + source])

        for source in range(2):
            halves = jnp.concatenate([halo[half, source, 0], halo[half, source, 1]], axis=0)
            unpack(half, 1 + source, halves, unpack_mat)

    def other_chip_landed(half):
        landed(field.at[half, pl.ds(12 - 11 * inl, 3), middle], cross_recv.at[half])

        @pl.when(has_right)
        def _():
            landed(corner.at[half, 1], cross_left_recv.at[half])

        @pl.when(has_left)
        def _():
            landed(corner.at[half, 0], cross_right_recv.at[half])

        halves = jnp.concatenate([corner[half, 0], corner[half, 1]], axis=0)
        unpack(half, 3 - 3 * inl, halves, unpack_corner)

    def one_product(half, turn):
        i = 4 + turn + inl * (7 - 2 * turn)
        grad_xl = dot32(diff_mat, field[half, i])
        grad_in = field[half, i + 1, cells].astype(jnp.float32) - field[
            half, i - 1, cells
        ].astype(jnp.float32)
        prods[half][0, i] = grad_in * grad_in
        prods[half][1, i] = grad_in * grad_xl
        prods[half][2, i] = grad_xl * grad_xl

    parts = []

    def slab_scores(half, turn):
        place = turn + inl * (1 - 2 * turn)
        base = 2 + place * il_rows
        slot = turn * 2 + half
        highs, lows = [], []
        for lanes in (slice(0, 128), slice(128, 256)):
            sums = [[] for _ in range(il_rows)]
            for which in range(3):
                p = [prods[half][which, base + r, :, lanes] for r in range(8)]
                a, b, c = p[1] + p[2], p[5] + p[6], p[3] + p[4]
                ac, bc = a + c, b + c
                box = box_mats[which == 1]
                for r, total in enumerate((p[0] + ac, p[5] + ac, p[2] + bc, p[7] + bc)):
                    high, low = split_bf16(total)
                    sums[r].append(dot32(box, high) + dot32(box, low))
            scores = []
            for s_ii, s_ix, s_xx in sums:
                total = s_ii + s_xx + 4.0 * epsilon
                gap = s_ii - s_xx
                scores.append(1.0 - (gap * gap + s_ix * s_ix) / (total * total))
            high, low = split_bf16(jnp.concatenate(scores, axis=0))
            highs.append(high)
            lows.append(low)
        high, low = jnp.concatenate(highs, axis=1), jnp.concatenate(lows, axis=1)
        nt = (((1,), (1,)), ((), ()))
        both = lax.dot_general(
            weight_mat, high, nt, preferred_element_type=jnp.float32
        ) + lax.dot_general(weight_mat, low, nt, preferred_element_type=jnp.float32)
        both = both[0:8]
        both = both + pltpu.roll(both, 4, 0)
        upper = lax.broadcasted_iota(jnp.int32, (8, 128), 0) < 4
        part_out[slot] = jnp.where(upper, both[:, 0:128], both[:, 128:256])
        part = pltpu.make_async_remote_copy(
            src_ref=part_out.at[slot],
            dst_ref=part_in.at[beta],
            send_sem=part_send.at[slot],
            recv_sem=part_recv.at[beta],
            device_id=device(half * 2 + core, inl * n_xl + place),
            device_id_type=MESH,
        )
        own = (half * 2 + core == beta) & (place == core)
        parts.append((part, own))

        @pl.when(own)
        def _():
            part_in[beta] = part_out[slot]

        @pl.when(jnp.logical_not(own))
        def _():
            part.start()

    for half in range(2):
        if half == 0:
            @pl.when(beta < n_band - 2)
            def _():
                pl.semaphore_wait(far_in, (n_band - 2 - beta) * 2)

        own_chip_landed(half)
        for turn in range(7):
            one_product(half, turn)
        slab_scores(half, 0)
        other_chip_landed(half)
        for turn in range(7, 10):
            one_product(half, turn)
        slab_scores(half, 1)

    for source in range(n_band):
        @pl.when(jnp.logical_not((beta % 2 == core) & (beta == source)))
        def _(source=source):
            pltpu.make_async_remote_copy(
                src_ref=part_out.at[0],
                dst_ref=part_in.at[source],
                send_sem=part_send.at[0],
                recv_sem=part_recv.at[source],
                device_id=device((beta + 1) % n_band, slab),
                device_id_type=MESH,
            ).wait_recv()

    for source in range(n_band):
        fault_ref[source] = part_in[source]

    for asked, copy in sent:
        @pl.when(asked)
        def _(copy=copy):
            copy.wait_send()

    for part, own in parts:
        @pl.when(jnp.logical_not(own))
        def _(part=part):
            part.wait_send()


def final_kernel(parts_ref, labels_ref, fault_ref, misfit_ref):
    first_half = lax.broadcasted_iota(jnp.int32, (8, 128), 1) < 64
    labels = labels_ref[...].astype(jnp.float32)
    halves = [[], []]
    for c in range(0, parts_ref.shape[0], 2):
        one, two = parts_ref[c], parts_ref[c + 1]
        halves[0].append(jnp.where(first_half, one, pltpu.roll(two, 64, 1)))
        halves[1].append(jnp.where(first_half, pltpu.roll(one, 64, 1), two))
    frames = fault_ref.shape[0]
    for odd in range(2):
        blocks = jnp.concatenate(halves[odd], axis=1)
        for two in range(2):
            i = two * 2 + odd
            here = blocks[two * 4 : two * 4 + 4]
            miss = jnp.tanh(here) - labels[i : i + 1]
            miss = miss * miss
            for f in range(frames):
                fault_ref[f, i : i + 1] = here[f : f + 1]
                misfit_ref[f, i : i + 1] = miss[f : f + 1]


def fused(traces, band_start, taper_len, band_weight, labels):
    il_rows, xl_cols, samples = traces.shape
    rows = il_rows * xl_cols
    n_band = lax.axis_size("band")
    slabs = lax.axis_size("inl") * lax.axis_size("xl")
    frames = FR // n_band
    out = jax.ShapeDtypeStruct((frames, il_rows, xl_cols * n_band), jnp.float32)
    vmem = pl.BlockSpec(memory_space=pltpu.VMEM)
    dma = pltpu.SemaphoreType.DMA
    parts = pl.pallas_call(
        functools.partial(fused_kernel, slabs, n_band),
        out_shape=jax.ShapeDtypeStruct((n_band, 8, 128), jnp.float32),
        in_specs=[pl.BlockSpec(memory_space=pltpu.HBM)] * 4,
        out_specs=vmem,
        scratch_shapes=[
            pltpu.VMEM((il_rows, xl_cols, samples), jnp.float32),
            pltpu.VMEM((rows, samples + 128), jnp.bfloat16),
            pltpu.VMEM((1, NB), jnp.int32),
            pltpu.VMEM((1, NB), jnp.int32),
            pltpu.VMEM((1, NB), jnp.float32),
            pltpu.VMEM((512, 4 * NB), jnp.bfloat16),
            pltpu.VMEM((14, rows, 2 * NB), jnp.float32),
            pltpu.VMEM((4, 16, xl_cols + EDGE, 4 * NB), jnp.bfloat16),
            pltpu.VMEM((4, 96, 4 * NB), jnp.bfloat16),
            pltpu.VMEM((2, 2, 2, 32, 4 * NB), jnp.bfloat16),
            pltpu.VMEM((2, 2, 16, 4 * NB), jnp.bfloat16),
            pltpu.VMEM((3, 16, xl_cols + 2 * RAD_XL, 4 * NB), jnp.float32),
            pltpu.VMEM((3, 16, xl_cols + 2 * RAD_XL, 4 * NB), jnp.float32),
            pltpu.VMEM((slabs, 8, 128), jnp.float32),
            pltpu.VMEM((n_band, 8, 128), jnp.float32),
            dma((samples // CHUNK,)),
            dma((3,)),
            dma((4,)),
            dma((2,)),
            dma((4,)),
            dma((4,)),
            dma((4,)),
            dma((4,)),
            dma((4,)),
            dma((2,)),
            dma((4,)),
            dma((2,)),
            dma((4,)),
            dma((2,)),
            dma((slabs,)),
            dma((n_band,)),
            pltpu.SemaphoreType.REGULAR,
        ],
        compiler_params=pltpu.CompilerParams(
            collective_id=0, has_side_effects=True, vmem_limit_bytes=32 * 1024 * 1024
        ),
    )(
        *[
            pltpu.with_memory_space_constraint(operand, pltpu.HBM)
            for operand in (
                traces,
                band_start.reshape(1, NB),
                taper_len.reshape(1, NB),
                band_weight.reshape(1, NB),
            )
        ]
    )
    return pl.pallas_call(
        final_kernel, out_shape=(out, out), in_specs=[vmem, vmem], out_specs=(vmem, vmem)
    )(
        pltpu.with_memory_space_constraint(parts, pltpu.VMEM),
        pltpu.with_memory_space_constraint(labels, pltpu.VMEM),
    )


def solution(mesh):
    shape = mesh.shape
    square = shape["band"] == 4 and shape["inl"] == 2 and shape["xl"] == 2
    return jax.shard_map(
        fused if square else on_device,
        mesh=mesh,
        in_specs=(
            P(("groups", "inl", "xl"), "band", None),
            P(),
            P(),
            P(),
            P(("groups", "inl", "xl"), None),
        ),
        out_specs=(
            P(("groups", "band"), ("inl", "xl"), None),
            P(("groups", "band"), ("inl", "xl"), None),
        ),
        check_vma=False,
    )
```

```python
import functools
import math

import jax
import jax.numpy as jnp
from jax import lax
from jax.experimental import pallas as pl
from jax.experimental.pallas import tpu as pltpu
from jax.sharding import PartitionSpec as P

WIN = 256
HOP = 64
FR = 16
NB = 64
RAD_INL = 2
RAD_XL = 4


epsilon = 1e-06


def with_halo(cells, sides, width):
    for axis, dim in sides:
        count = lax.axis_size(axis)
        ends = count - 1
        head = lax.slice_in_dim(cells, 0, width, axis=dim)
        tail = lax.slice_in_dim(cells, cells.shape[dim] - width, cells.shape[dim], axis=dim)
        cells = jnp.concatenate(
            [
                lax.ppermute(tail, axis, [(i, (i + 1) % count) for i in range(ends)]),
                cells,
                lax.ppermute(head, axis, [((i + 1) % count, i) for i in range(ends)]),
            ],
            axis=dim,
        )
    return cells


def wave_values(offsets, band_ids, taper_lens):
    shifted = offsets.astype(jnp.float32)
    ramp_len = taper_lens.astype(jnp.float32) + 1.0
    tapers = jnp.minimum(jnp.minimum((shifted + 1.0) / ramp_len, (WIN - shifted) / ramp_len), 1.0)
    cycles = (band_ids + 1) * offsets % WIN
    angles = cycles.astype(jnp.float32) * (2.0 * math.pi / WIN)
    return (tapers * jnp.cos(angles), tapers * jnp.sin(angles))


def band_coeffs(trace_rows, band_start, taper_len):
    row_total = trace_rows.shape[0]
    samples = trace_rows.shape[1]
    per_group = 8
    time_ids = jnp.arange(samples, dtype=jnp.int32)
    frame_ids = jnp.arange(FR, dtype=jnp.int32)

    def one_group(inputs):
        starts, tapers_in, band_ids = inputs
        offsets = time_ids[None, None, :] - starts[:, None, None] - frame_ids[None, :, None] * HOP
        valid = (offsets >= 0) & (offsets < WIN)
        clipped = jnp.clip(offsets, 0, WIN - 1)
        cosine, sine_part = wave_values(clipped, band_ids[:, None, None], tapers_in[:, None, None])
        kernel = jnp.stack([cosine, sine_part], axis=1)
        kernel = jnp.where(valid[:, None], kernel, 0.0).astype(jnp.bfloat16)
        kernel = kernel.reshape(per_group * 2 * FR, samples)
        return lax.dot_general(
            kernel, trace_rows, (((1,), (1,)), ((), ())), preferred_element_type=jnp.float32
        )

    group_count = NB // per_group
    grouped = lax.map(
        one_group,
        (
            band_start.reshape(group_count, per_group),
            taper_len.reshape(group_count, per_group),
            jnp.arange(NB, dtype=jnp.int32).reshape(group_count, per_group),
        ),
    )
    return grouped.reshape(NB, 2, FR, row_total)


def coherence(s_ii, s_ix, s_xx):
    return ((s_ii - s_xx) ** 2 + 4.0 * s_ix**2) / (s_ii + s_xx + epsilon) ** 2


def column_work(conc_block, band_weight):
    xl_cols = conc_block.shape[3]
    row_count = conc_block.shape[2]
    extended = with_halo(conc_block, (("band", 3),), RAD_XL + 1)
    field_f32 = extended.astype(jnp.float32)
    rows_pad = jnp.pad(field_f32, ((0, 0), (0, 0), (1, 1), (0, 0)))
    grad_in = 0.5 * (rows_pad[:, :, 2:, 1:-1] - rows_pad[:, :, :-2, 1:-1])
    grad_xl = 0.5 * (field_f32[..., 2:] - field_f32[..., :-2])
    col_count = grad_xl.shape[3]
    global_cols = lax.axis_index("band") * xl_cols - RAD_XL + jnp.arange(col_count, dtype=jnp.int32)
    inside = ((global_cols >= 0) & (global_cols < xl_cols * lax.axis_size("band"))).astype(
        jnp.float32
    )
    grad_in = grad_in * inside
    grad_xl = grad_xl * inside
    smoothed = []
    for product in (grad_in * grad_in, grad_in * grad_xl, grad_xl * grad_xl):
        inl_pad = jnp.pad(product, ((0, 0), (0, 0), (RAD_INL, RAD_INL), (0, 0)))
        inline_sum = inl_pad[:, :, 0:row_count]
        for offset in range(1, 2 * RAD_INL + 1):
            inline_sum = inline_sum + inl_pad[:, :, offset : offset + row_count]
        summed = inline_sum[..., 0:xl_cols]
        for offset in range(1, 2 * RAD_XL + 1):
            summed = summed + inline_sum[..., offset : offset + xl_cols]
        smoothed.append(summed)
    scores = band_weight[:, None, None, None] * (
        1.0 - coherence(smoothed[0], smoothed[1], smoothed[2])
    )
    return jnp.sum(scores, axis=0)


def on_device(traces, band_start, taper_len, band_weight, labels):
    il_rows, xl_cols, samples = traces.shape
    trace_rows = traces.reshape(il_rows * xl_cols, samples).astype(jnp.bfloat16)
    coeffs = band_coeffs(trace_rows, band_start, taper_len)
    coeffs = coeffs.reshape(NB, 2, FR, il_rows, xl_cols)
    band_power = coeffs[:, 0] ** 2 + coeffs[:, 1] ** 2
    amplitude = jnp.log(1.0 + band_power)
    average = jnp.mean(amplitude, axis=0, keepdims=True)
    concentration = (amplitude / (1.0 + average)).astype(jnp.bfloat16)
    spread = lax.all_to_all(concentration, ("inl", "xl"), split_axis=1, concat_axis=2, tiled=True)
    partial_cols = column_work(spread, band_weight)
    by_slab = lax.all_to_all(partial_cols, ("inl", "xl"), split_axis=1, concat_axis=0, tiled=True)
    fault_map = lax.all_to_all(by_slab, "band", split_axis=0, concat_axis=2, tiled=True)
    misfit = (jnp.tanh(fault_map) - labels.astype(jnp.float32)[None]) ** 2
    return (fault_map, misfit)


MESH = pl.DeviceIdType.MESH
EDGE = 16
CHUNK = 512
HALO = RAD_XL + 1


def wave_block(first, start, taper, rows):
    lane = lax.broadcasted_iota(jnp.int32, (rows, 2 * NB), 1)
    late = (lane >= NB).astype(jnp.int32)
    time = lax.broadcasted_iota(jnp.int32, (rows, 2 * NB), 0) + first
    band = lane - late * NB
    lag = time - (start & 127) + late * HOP
    valid = (lag >= 0) & (lag < WIN)
    lag_f = lag.astype(jnp.float32)
    tapers = jnp.minimum(
        jnp.minimum(lag_f + 1.0, WIN - lag_f) / (taper.astype(jnp.float32) + 1.0), 1.0
    )
    tapers = jnp.where(valid, tapers, 0.0)
    cycles = ((band + 1) * lag) & (WIN - 1)
    quarter = (cycles + 32) >> 6
    x = (cycles - quarter * 64).astype(jnp.float32) * (2.0 * math.pi / WIN)
    z = x * x
    sin_x = x + x * z * (-1.6666654611e-1 + z * (8.3321608736e-3 + z * -1.9515295891e-4))
    cos_x = (1.0 - 0.5 * z) + z * z * (
        4.166664568298827e-2 + z * (-1.388731625493765e-3 + z * 2.443315711809948e-5)
    )
    swap = (quarter & 1) == 1
    cos_sign = jnp.where(((quarter + 1) & 2) == 2, -tapers, tapers)
    sin_sign = jnp.where((quarter & 2) == 2, -tapers, tapers)
    cosine = cos_sign * jnp.where(swap, sin_x, cos_x)
    sine = sin_sign * jnp.where(swap, cos_x, sin_x)
    return cosine, sine


def split_bf16(x):
    high = x.astype(jnp.bfloat16)
    return high, (x - high.astype(jnp.float32)).astype(jnp.bfloat16)


def dot32(a, b):
    return jnp.dot(a, b, preferred_element_type=jnp.float32)


def twice(x):
    return jnp.concatenate([x, x], axis=1)


def fused_kernel(
    slabs, n_band, traces, start_ref, taper_ref, weight_ref, fault_ref,
    t32, tb, start_at, taper_at, weight_at,
    waves, power, field, packed, halo, corner, prods_0, prods_1, part_out, part_in,
    load_sem, small_sem, main_send, main_recv, left_send, left_recv, right_send, right_recv,
    cross_send, cross_recv, cross_left_send, cross_left_recv, cross_right_send,
    cross_right_recv, part_send, part_recv, far_in,
):
    group = lax.axis_index("groups")
    beta = lax.axis_index("band")
    n_xl = lax.axis_size("xl")
    inl = lax.axis_index("inl")
    core = lax.axis_index("xl")
    slab = inl * n_xl + core
    il_rows, xl_cols = traces.shape[0], traces.shape[1]
    rows = il_rows * xl_cols

    def device(band_at, slab_at):
        return (group, band_at, slab_at // n_xl, slab_at % n_xl)

    smalls = [
        pltpu.make_async_copy(source, to, small_sem.at[i])
        for i, (source, to) in enumerate(
            (
                (start_ref, start_at),
                (taper_ref, taper_at),
                (weight_ref, weight_at),
            )
        )
    ]
    for small in smalls:
        small.start()
    loads = [
        pltpu.make_async_copy(
            traces.at[:, :, pl.ds(i * CHUNK, CHUNK)],
            t32.at[:, :, pl.ds(i * CHUNK, CHUNK)],
            load_sem.at[i],
        )
        for i in range(traces.shape[2] // CHUNK)
    ]
    for load in loads:
        load.start()

    barrier = pltpu.get_barrier_semaphore()
    for to_band in range(n_band):
        for ds in range(slabs):
            @pl.when((to_band >= beta - 1) & ((to_band != beta) | (ds > 0)))
            def _(to_band=to_band, ds=ds):
                pl.semaphore_signal(
                    barrier,
                    inc=1,
                    device_id=device(to_band, (slab + ds) % slabs),
                    device_id_type=MESH,
                )

    entered = jnp.minimum(beta + 2, n_band) * slabs - 1

    field[0:2, 3 + 9 * inl] = jnp.zeros((2,) + field.shape[2:], field.dtype)
    @pl.when(beta == 0)
    def _():
        halo[:, :, 0] = jnp.zeros((2, n_xl) + halo.shape[3:], halo.dtype)
        corner[:, 0] = jnp.zeros((2,) + corner.shape[2:], corner.dtype)

    @pl.when(beta == n_band - 1)
    def _():
        halo[:, :, 1] = jnp.zeros((2, n_xl) + halo.shape[3:], halo.dtype)
        corner[:, 1] = jnp.zeros((2,) + corner.shape[2:], corner.dtype)

    prods = (prods_0, prods_1)
    for half in range(2):
        for row in range(2):
            prods[half][:, 2 + row + 10 * inl] = jnp.zeros((3,) + prods_0.shape[2:], jnp.float32)

    half_r = lax.broadcasted_iota(jnp.int32, (2 * NB, 2 * NB), 0) // NB
    half_c = lax.broadcasted_iota(jnp.int32, (2 * NB, 2 * NB), 1) // NB
    mean_mat = jnp.where(half_r == half_c, 1.0 / NB, 0.0).astype(jnp.bfloat16)

    mean_mat = jnp.concatenate([mean_mat, mean_mat], axis=0)
    def one_hot(ones):
        return jnp.where(ones, 1.0, 0.0).astype(jnp.bfloat16)

    out_at = lax.broadcasted_iota(jnp.int32, (96, 8 * EDGE), 0)
    in_at = lax.broadcasted_iota(jnp.int32, (96, 8 * EDGE), 1)
    from_right = in_at // (4 * EDGE)
    in_row = in_at % (4 * EDGE) // EDGE
    in_col = in_at % EDGE - from_right * (EDGE - HALO)
    in_code = jnp.where(
        (in_col >= 0) & (in_col < HALO), from_right * 64 + in_row * HALO + in_col, -2
    )
    corner_code = jnp.where(
        out_at % 16 < 3 * HALO, out_at // 16 % 2 * 64 + out_at % 16 + (1 - inl) * HALO, -1
    )
    out_code = jnp.where(out_at < 64, out_at // 32 * 64 + out_at % 32, corner_code)
    pack_mat = one_hot(in_code == out_code)

    def column_of(place):
        near = jnp.where(place < xl_cols + RAD_XL, place - xl_cols - RAD_XL, place - RAD_XL)
        far = jnp.where(
            place < xl_cols + 2 * RAD_XL + 2,
            jnp.where(place == xl_cols + 2 * RAD_XL, -HALO, xl_cols + RAD_XL),
            4 * xl_cols,
        )
        return jnp.where(
            place < xl_cols, place, jnp.where(place < xl_cols + 2 * RAD_XL, near, far)
        )

    def unpack_matrix(depth, first):
        to = lax.broadcasted_iota(jnp.int32, (4 * EDGE, 2 * depth), 0)
        at = lax.broadcasted_iota(jnp.int32, (4 * EDGE, 2 * depth), 1)
        column = column_of(xl_cols + to % EDGE)
        row = to // EDGE - first
        west = (at < depth) & (column < 0) & (at == row * HALO + column + HALO)
        east = (at >= depth) & (column < 2 * xl_cols) & (
            at - depth == row * HALO + column - xl_cols
        )
        fits = (row >= 0) & (row < 4)
        return one_hot(fits & (west | ((column >= xl_cols) & east)))

    unpack_mat = unpack_matrix(32, 0)
    unpack_corner = unpack_matrix(16, inl)

    wide = xl_cols + 2 * RAD_XL
    cells = pl.ds(0, wide)
    shape = (wide, xl_cols + EDGE)
    out_x = column_of(lax.broadcasted_iota(jnp.int32, shape, 0))
    in_x = column_of(lax.broadcasted_iota(jnp.int32, shape, 1))
    diff_mat = (
        (in_x == out_x + 1).astype(jnp.float32) - (in_x == out_x - 1).astype(jnp.float32)
    ).astype(jnp.bfloat16)
    out_x = lax.broadcasted_iota(jnp.int32, (xl_cols, wide), 0)
    in_x = column_of(lax.broadcasted_iota(jnp.int32, (xl_cols, wide), 1))
    at_x = in_x + beta * xl_cols
    near = (jnp.abs(in_x - out_x) <= RAD_XL) & (at_x >= 0) & (at_x < xl_cols * n_band)
    box_mat = near.astype(jnp.float32)
    box_mats = [box_mat.astype(jnp.bfloat16), (2.0 * box_mat).astype(jnp.bfloat16)]
    for small in smalls:
        small.wait()
    start = twice(start_at[...])
    taper = twice(taper_at[...])
    early = lax.broadcasted_iota(jnp.int32, (HOP, 2 * NB), 1) < NB
    last = [jnp.zeros((HOP, 2 * NB), jnp.float32)] * 2
    for first in range(0, 512, 2 * HOP):
        now = wave_block(first, start, taper, HOP)
        for i in range(2):
            lanes = slice(i * 2 * NB, (i + 1) * 2 * NB)
            waves[first : first + HOP, lanes] = jnp.where(early, now[i], last[i]).astype(
                jnp.bfloat16
            )
            waves[first + HOP : first + 2 * HOP, lanes] = pltpu.roll(now[i], NB, 1).astype(
                jnp.bfloat16
            )
        last = now
    samples = traces.shape[2]
    tb[:, samples:] = jnp.zeros((rows, 128), jnp.bfloat16)

    def land(chunk):
        loads[chunk].wait()
        span = slice(chunk * CHUNK, (chunk + 1) * CHUNK)
        tb[:, span] = t32[:, :, span].reshape(rows, CHUNK).astype(jnp.bfloat16)

    def one_step(step):
        if step % 4 == 1 and step < 13:
            land(step // 4 + 1)
        at = step * 128
        coeffs = dot32(tb[:, pl.ds(at, 512)], waves[...])
        cosine, sine = coeffs[:, 0 : 2 * NB], coeffs[:, 2 * NB :]
        power[step] = cosine * cosine + sine * sine

    land(0)

    first_step = start >> 7
    def concentrations(m, slot):
        for j in range(2):
            pair = m * 2 + j
            chosen = power[pair]
            for q in range(1, 7):
                chosen = jnp.where(first_step == q, power[pair + q], chosen)
            amplitude = jnp.log(1.0 + chosen)
            average = dot32(jnp.concatenate(split_bf16(amplitude), axis=1), mean_mat)
            value = (amplitude / (1.0 + average)).astype(jnp.bfloat16)
            field[slot, mine, middle, j * 2 * NB : (j + 1) * 2 * NB] = value.reshape(
                il_rows, xl_cols, 2 * NB
            )

    mine = pl.ds(4 + core * il_rows, il_rows)
    border_from = pl.ds(4 + core * il_rows + 1 - inl, 3)
    border_to = pl.ds(1 + 11 * inl, 3)
    at_border = core == 1 - inl
    middle = pl.ds(0, xl_cols)
    first_cols, last_cols = pl.ds(0, EDGE), pl.ds(xl_cols - EDGE, EDGE)
    left_band, right_band = (beta + n_band - 1) % n_band, (beta + 1) % n_band
    has_left, has_right = beta > 0, beta < n_band - 1

    def place_of(m):
        owner, half = m % 2, m // 2
        return owner, half, half + 2 * ((core + owner) % 2)

    def pack(m):
        _, _, slot = place_of(m)
        edges = jnp.concatenate(
            [
                field[slot, mine, first_cols].reshape(4 * EDGE, 4 * NB),
                field[slot, mine, last_cols].reshape(4 * EDGE, 4 * NB),
            ],
            axis=0,
        )
        packed[m] = dot32(pack_mat, edges).astype(jnp.bfloat16)

    def unpack(half, block, halves, matrix):
        edges = dot32(matrix, halves).astype(jnp.bfloat16)
        field[half, pl.ds(4 * block, 4), pl.ds(xl_cols, EDGE)] = edges.reshape(4, EDGE, 4 * NB)

    sent = []

    def send(asked, source, to, send_sem, recv_sem, band_at, slab_at):
        copy = pltpu.make_async_remote_copy(
            src_ref=source,
            dst_ref=to,
            send_sem=send_sem,
            recv_sem=recv_sem,
            device_id=device(band_at, slab_at),
            device_id_type=MESH,
        )
        sent.append((asked, copy))

        @pl.when(asked)
        def _():
            copy.start()

    def send_all(m):
        owner, half, slot = place_of(m)
        own_chip, other_chip = inl * n_xl + owner, (1 - inl) * n_xl + owner
        send(at_border, field.at[slot, border_from, middle], field.at[half, border_to, middle],
             cross_send.at[m], cross_recv.at[half], beta, other_chip)
        send(core == 1 - owner, field.at[slot, mine, middle], field.at[half, mine, middle],
             main_send.at[m], main_recv.at[half], beta, own_chip)
        send(has_left, packed.at[m, pl.ds(0, 32)], halo.at[half, core, 1],
             left_send.at[m], left_recv.at[half * 2 + core], left_band, own_chip)
        send(has_right, packed.at[m, pl.ds(32, 32)], halo.at[half, core, 0],
             right_send.at[m], right_recv.at[half * 2 + core], right_band, own_chip)
        send(at_border & has_left, packed.at[m, pl.ds(64, 16)], corner.at[half, 1],
             cross_left_send.at[m], cross_left_recv.at[half], left_band, other_chip)
        send(at_border & has_right, packed.at[m, pl.ds(80, 16)], corner.at[half, 0],
             cross_right_send.at[m], cross_right_recv.at[half], right_band, other_chip)

    for step in range(8):
        one_step(step)
    for m in range(4):
        for step in (range(0), range(8, 12), range(12, 14), range(0))[m]:
            one_step(step)
        concentrations(m, place_of(m)[2])
        if m == 0:
            pl.semaphore_wait(barrier, entered)

            for to_band in range(n_band - 2):
                @pl.when(beta >= to_band + 2)
                def _(to_band=to_band):
                    for to_core in range(2):
                        pl.semaphore_signal(
                            far_in,
                            inc=1,
                            device_id=device(to_band, inl * n_xl + to_core),
                            device_id_type=MESH,
                        )

        pack(m)
        send_all(m)

    weights = twice(twice(weight_at[...]))
    row = lax.broadcasted_iota(jnp.int32, (16, 4 * NB), 0)
    lane = lax.broadcasted_iota(jnp.int32, (16, 4 * NB), 1)
    w_high, w_low = split_bf16(weights)
    w_high = w_high.astype(jnp.float32)
    w_low = w_low.astype(jnp.float32)
    weight_mat = jnp.where(
        row == lane // NB, w_high, jnp.where(row - 4 == lane // NB, w_low, 0.0)
    ).astype(jnp.bfloat16)

    def landed(block, sem):
        pltpu.make_async_remote_copy(
            src_ref=block,
            dst_ref=block,
            send_sem=main_send.at[0],
            recv_sem=sem,
            device_id=device(beta, inl * n_xl + 1 - core),
            device_id_type=MESH,
        ).wait_recv()

    def own_chip_landed(half):
        landed(
            field.at[half, pl.ds(4 + (1 - core) * il_rows, il_rows), middle], main_recv.at[half]
        )

        @pl.when(has_right)
        def _():
            for source in range(2):
                landed(halo.at[half, source, 1], left_recv.at[half * 2 + source])

        @pl.when(has_left)
        def _():
            for source in range(2):
                landed(halo.at[half, source, 0], right_recv.at[half * 2 + source])

        for source in range(2):
            halves = jnp.concatenate([halo[half, source, 0], halo[half, source, 1]], axis=0)
            unpack(half, 1 + source, halves, unpack_mat)

    def other_chip_landed(half):
        landed(field.at[half, pl.ds(12 - 11 * inl, 3), middle], cross_recv.at[half])

        @pl.when(has_right)
        def _():
            landed(corner.at[half, 1], cross_left_recv.at[half])

        @pl.when(has_left)
        def _():
            landed(corner.at[half, 0], cross_right_recv.at[half])

        halves = jnp.concatenate([corner[half, 0], corner[half, 1]], axis=0)
        unpack(half, 3 - 3 * inl, halves, unpack_corner)

    def one_product(half, turn):
        i = 4 + turn + inl * (7 - 2 * turn)
        grad_xl = dot32(diff_mat, field[half, i])
        grad_in = field[half, i + 1, cells].astype(jnp.float32) - field[
            half, i - 1, cells
        ].astype(jnp.float32)
        prods[half][0, i] = grad_in * grad_in
        prods[half][1, i] = grad_in * grad_xl
        prods[half][2, i] = grad_xl * grad_xl

    parts = []

    def slab_scores(half, turn):
        place = turn + inl * (1 - 2 * turn)
        base = 2 + place * il_rows
        slot = turn * 2 + half
        sums = [[] for _ in range(il_rows)]
        for which in range(3):
            p = [prods[half][which, base + r] for r in range(8)]
            a, b, c = p[1] + p[2], p[5] + p[6], p[3] + p[4]
            ac, bc = a + c, b + c
            box = box_mats[which == 1]
            for r, total in enumerate((p[0] + ac, p[5] + ac, p[2] + bc, p[7] + bc)):
                high, low = split_bf16(total)
                sums[r].append(dot32(box, high) + dot32(box, low))
        scores = []
        for s_ii, s_ix, s_xx in sums:
            total = s_ii + s_xx + 4.0 * epsilon
            gap = s_ii - s_xx
            scores.append(1.0 - (gap * gap + s_ix * s_ix) / (total * total))
        high, low = split_bf16(jnp.concatenate(scores, axis=0))
        nt = (((1,), (1,)), ((), ()))
        both = lax.dot_general(
            weight_mat, high, nt, preferred_element_type=jnp.float32
        ) + lax.dot_general(weight_mat, low, nt, preferred_element_type=jnp.float32)
        both = both[0:8]
        both = both + pltpu.roll(both, 4, 0)
        upper = lax.broadcasted_iota(jnp.int32, (8, 128), 0) < 4
        part_out[slot] = jnp.where(upper, both[:, 0:128], both[:, 128:256])
        part = pltpu.make_async_remote_copy(
            src_ref=part_out.at[slot],
            dst_ref=part_in.at[beta],
            send_sem=part_send.at[slot],
            recv_sem=part_recv.at[beta],
            device_id=device(half * 2 + core, inl * n_xl + place),
            device_id_type=MESH,
        )
        own = (half * 2 + core == beta) & (place == core)
        parts.append((part, own))

        @pl.when(own)
        def _():
            part_in[beta] = part_out[slot]

        @pl.when(jnp.logical_not(own))
        def _():
            part.start()

    for half in range(2):
        if half == 0:
            @pl.when(beta < n_band - 2)
            def _():
                pl.semaphore_wait(far_in, (n_band - 2 - beta) * 2)

        own_chip_landed(half)
        for turn in range(7):
            one_product(half, turn)
        slab_scores(half, 0)
        other_chip_landed(half)
        for turn in range(7, 10):
            one_product(half, turn)
        slab_scores(half, 1)

    for asked, copy in sent:
        @pl.when(asked)
        def _(copy=copy):
            copy.wait_send()

    for source in range(n_band):
        @pl.when(jnp.logical_not((beta % 2 == core) & (beta == source)))
        def _(source=source):
            pltpu.make_async_remote_copy(
                src_ref=part_out.at[0],
                dst_ref=part_in.at[source],
                send_sem=part_send.at[0],
                recv_sem=part_recv.at[source],
                device_id=device((beta + 1) % n_band, slab),
                device_id_type=MESH,
            ).wait_recv()

    for source in range(n_band):
        fault_ref[source] = part_in[source]

    for part, own in parts:
        @pl.when(jnp.logical_not(own))
        def _(part=part):
            part.wait_send()


def final_kernel(parts_ref, labels_ref, fault_ref, misfit_ref):
    first_half = lax.broadcasted_iota(jnp.int32, (8, 128), 1) < 64
    labels = labels_ref[...].astype(jnp.float32)
    halves = [[], []]
    for c in range(0, parts_ref.shape[0], 2):
        one, two = parts_ref[c], parts_ref[c + 1]
        halves[0].append(jnp.where(first_half, one, pltpu.roll(two, 64, 1)))
        halves[1].append(jnp.where(first_half, pltpu.roll(one, 64, 1), two))
    frames = fault_ref.shape[0]
    for odd in range(2):
        blocks = jnp.concatenate(halves[odd], axis=1)
        for two in range(2):
            i = two * 2 + odd
            here = blocks[two * 4 : two * 4 + 4]
            miss = jnp.tanh(here) - labels[i : i + 1]
            miss = miss * miss
            for f in range(frames):
                fault_ref[f, i : i + 1] = here[f : f + 1]
                misfit_ref[f, i : i + 1] = miss[f : f + 1]


def fused(traces, band_start, taper_len, band_weight, labels):
    il_rows, xl_cols, samples = traces.shape
    rows = il_rows * xl_cols
    n_band = lax.axis_size("band")
    slabs = lax.axis_size("inl") * lax.axis_size("xl")
    frames = FR // n_band
    out = jax.ShapeDtypeStruct((frames, il_rows, xl_cols * n_band), jnp.float32)
    vmem = pl.BlockSpec(memory_space=pltpu.VMEM)
    dma = pltpu.SemaphoreType.DMA
    parts = pl.pallas_call(
        functools.partial(fused_kernel, slabs, n_band),
        out_shape=jax.ShapeDtypeStruct((n_band, 8, 128), jnp.float32),
        in_specs=[pl.BlockSpec(memory_space=pltpu.HBM)] * 4,
        out_specs=vmem,
        scratch_shapes=[
            pltpu.VMEM((il_rows, xl_cols, samples), jnp.float32),
            pltpu.VMEM((rows, samples + 128), jnp.bfloat16),
            pltpu.VMEM((1, NB), jnp.int32),
            pltpu.VMEM((1, NB), jnp.int32),
            pltpu.VMEM((1, NB), jnp.float32),
            pltpu.VMEM((512, 4 * NB), jnp.bfloat16),
            pltpu.VMEM((14, rows, 2 * NB), jnp.float32),
            pltpu.VMEM((4, 16, xl_cols + EDGE, 4 * NB), jnp.bfloat16),
            pltpu.VMEM((4, 96, 4 * NB), jnp.bfloat16),
            pltpu.VMEM((2, 2, 2, 32, 4 * NB), jnp.bfloat16),
            pltpu.VMEM((2, 2, 16, 4 * NB), jnp.bfloat16),
            pltpu.VMEM((3, 16, xl_cols + 2 * RAD_XL, 4 * NB), jnp.float32),
            pltpu.VMEM((3, 16, xl_cols + 2 * RAD_XL, 4 * NB), jnp.float32),
            pltpu.VMEM((slabs, 8, 128), jnp.float32),
            pltpu.VMEM((n_band, 8, 128), jnp.float32),
            dma((samples // CHUNK,)),
            dma((3,)),
            dma((4,)),
            dma((2,)),
            dma((4,)),
            dma((4,)),
            dma((4,)),
            dma((4,)),
            dma((4,)),
            dma((2,)),
            dma((4,)),
            dma((2,)),
            dma((4,)),
            dma((2,)),
            dma((slabs,)),
            dma((n_band,)),
            pltpu.SemaphoreType.REGULAR,
        ],
        compiler_params=pltpu.CompilerParams(
            collective_id=0, has_side_effects=True, vmem_limit_bytes=32 * 1024 * 1024
        ),
    )(
        *[
            pltpu.with_memory_space_constraint(operand, pltpu.HBM)
            for operand in (
                traces,
                band_start.reshape(1, NB),
                taper_len.reshape(1, NB),
                band_weight.reshape(1, NB),
            )
        ]
    )
    return pl.pallas_call(
        final_kernel, out_shape=(out, out), in_specs=[vmem, vmem], out_specs=(vmem, vmem)
    )(
        pltpu.with_memory_space_constraint(parts, pltpu.VMEM),
        pltpu.with_memory_space_constraint(labels, pltpu.VMEM),
    )


def solution(mesh):
    shape = mesh.shape
    square = shape["band"] == 4 and shape["inl"] == 2 and shape["xl"] == 2
    return jax.shard_map(
        fused if square else on_device,
        mesh=mesh,
        in_specs=(
            P(("groups", "inl", "xl"), "band", None),
            P(),
            P(),
            P(),
            P(("groups", "inl", "xl"), None),
        ),
        out_specs=(
            P(("groups", "band"), ("inl", "xl"), None),
            P(("groups", "band"), ("inl", "xl"), None),
        ),
        check_vma=False,
    )
```

```python
import functools
import math

import jax
import jax.numpy as jnp
from jax import lax
from jax.experimental import pallas as pl
from jax.experimental.pallas import tpu as pltpu
from jax.sharding import PartitionSpec as P

WIN = 256
HOP = 64
FR = 16
NB = 64
RAD_INL = 2
RAD_XL = 4


epsilon = 1e-06


def with_halo(cells, sides, width):
    for axis, dim in sides:
        count = lax.axis_size(axis)
        ends = count - 1
        head = lax.slice_in_dim(cells, 0, width, axis=dim)
        tail = lax.slice_in_dim(cells, cells.shape[dim] - width, cells.shape[dim], axis=dim)
        cells = jnp.concatenate(
            [
                lax.ppermute(tail, axis, [(i, (i + 1) % count) for i in range(ends)]),
                cells,
                lax.ppermute(head, axis, [((i + 1) % count, i) for i in range(ends)]),
            ],
            axis=dim,
        )
    return cells


def wave_values(offsets, band_ids, taper_lens):
    shifted = offsets.astype(jnp.float32)
    ramp_len = taper_lens.astype(jnp.float32) + 1.0
    tapers = jnp.minimum(jnp.minimum((shifted + 1.0) / ramp_len, (WIN - shifted) / ramp_len), 1.0)
    cycles = (band_ids + 1) * offsets % WIN
    angles = cycles.astype(jnp.float32) * (2.0 * math.pi / WIN)
    return (tapers * jnp.cos(angles), tapers * jnp.sin(angles))


def band_coeffs(trace_rows, band_start, taper_len):
    row_total = trace_rows.shape[0]
    samples = trace_rows.shape[1]
    per_group = 8
    time_ids = jnp.arange(samples, dtype=jnp.int32)
    frame_ids = jnp.arange(FR, dtype=jnp.int32)

    def one_group(inputs):
        starts, tapers_in, band_ids = inputs
        offsets = time_ids[None, None, :] - starts[:, None, None] - frame_ids[None, :, None] * HOP
        valid = (offsets >= 0) & (offsets < WIN)
        clipped = jnp.clip(offsets, 0, WIN - 1)
        cosine, sine_part = wave_values(clipped, band_ids[:, None, None], tapers_in[:, None, None])
        kernel = jnp.stack([cosine, sine_part], axis=1)
        kernel = jnp.where(valid[:, None], kernel, 0.0).astype(jnp.bfloat16)
        kernel = kernel.reshape(per_group * 2 * FR, samples)
        return lax.dot_general(
            kernel, trace_rows, (((1,), (1,)), ((), ())), preferred_element_type=jnp.float32
        )

    group_count = NB // per_group
    grouped = lax.map(
        one_group,
        (
            band_start.reshape(group_count, per_group),
            taper_len.reshape(group_count, per_group),
            jnp.arange(NB, dtype=jnp.int32).reshape(group_count, per_group),
        ),
    )
    return grouped.reshape(NB, 2, FR, row_total)


def coherence(s_ii, s_ix, s_xx):
    return ((s_ii - s_xx) ** 2 + 4.0 * s_ix**2) / (s_ii + s_xx + epsilon) ** 2


def column_work(conc_block, band_weight):
    xl_cols = conc_block.shape[3]
    row_count = conc_block.shape[2]
    extended = with_halo(conc_block, (("band", 3),), RAD_XL + 1)
    field_f32 = extended.astype(jnp.float32)
    rows_pad = jnp.pad(field_f32, ((0, 0), (0, 0), (1, 1), (0, 0)))
    grad_in = 0.5 * (rows_pad[:, :, 2:, 1:-1] - rows_pad[:, :, :-2, 1:-1])
    grad_xl = 0.5 * (field_f32[..., 2:] - field_f32[..., :-2])
    col_count = grad_xl.shape[3]
    global_cols = lax.axis_index("band") * xl_cols - RAD_XL + jnp.arange(col_count, dtype=jnp.int32)
    inside = ((global_cols >= 0) & (global_cols < xl_cols * lax.axis_size("band"))).astype(
        jnp.float32
    )
    grad_in = grad_in * inside
    grad_xl = grad_xl * inside
    smoothed = []
    for product in (grad_in * grad_in, grad_in * grad_xl, grad_xl * grad_xl):
        inl_pad = jnp.pad(product, ((0, 0), (0, 0), (RAD_INL, RAD_INL), (0, 0)))
        inline_sum = inl_pad[:, :, 0:row_count]
        for offset in range(1, 2 * RAD_INL + 1):
            inline_sum = inline_sum + inl_pad[:, :, offset : offset + row_count]
        summed = inline_sum[..., 0:xl_cols]
        for offset in range(1, 2 * RAD_XL + 1):
            summed = summed + inline_sum[..., offset : offset + xl_cols]
        smoothed.append(summed)
    scores = band_weight[:, None, None, None] * (
        1.0 - coherence(smoothed[0], smoothed[1], smoothed[2])
    )
    return jnp.sum(scores, axis=0)


def on_device(traces, band_start, taper_len, band_weight, labels):
    il_rows, xl_cols, samples = traces.shape
    trace_rows = traces.reshape(il_rows * xl_cols, samples).astype(jnp.bfloat16)
    coeffs = band_coeffs(trace_rows, band_start, taper_len)
    coeffs = coeffs.reshape(NB, 2, FR, il_rows, xl_cols)
    band_power = coeffs[:, 0] ** 2 + coeffs[:, 1] ** 2
    amplitude = jnp.log(1.0 + band_power)
    average = jnp.mean(amplitude, axis=0, keepdims=True)
    concentration = (amplitude / (1.0 + average)).astype(jnp.bfloat16)
    spread = lax.all_to_all(concentration, ("inl", "xl"), split_axis=1, concat_axis=2, tiled=True)
    partial_cols = column_work(spread, band_weight)
    by_slab = lax.all_to_all(partial_cols, ("inl", "xl"), split_axis=1, concat_axis=0, tiled=True)
    fault_map = lax.all_to_all(by_slab, "band", split_axis=0, concat_axis=2, tiled=True)
    misfit = (jnp.tanh(fault_map) - labels.astype(jnp.float32)[None]) ** 2
    return (fault_map, misfit)


MESH = pl.DeviceIdType.MESH
EDGE = 16
CHUNK = 512
HALO = RAD_XL + 1


def wave_block(first, start, taper, rows):
    lane = lax.broadcasted_iota(jnp.int32, (rows, 2 * NB), 1)
    late = (lane >= NB).astype(jnp.int32)
    time = lax.broadcasted_iota(jnp.int32, (rows, 2 * NB), 0) + first
    band = lane - late * NB
    lag = time - (start & 127) + late * HOP
    valid = (lag >= 0) & (lag < WIN)
    lag_f = lag.astype(jnp.float32)
    tapers = jnp.minimum(
        jnp.minimum(lag_f + 1.0, WIN - lag_f) / (taper.astype(jnp.float32) + 1.0), 1.0
    )
    tapers = jnp.where(valid, tapers, 0.0)
    cycles = ((band + 1) * lag) & (WIN - 1)
    quarter = (cycles + 32) >> 6
    x = (cycles - quarter * 64).astype(jnp.float32) * (2.0 * math.pi / WIN)
    z = x * x
    sin_x = x + x * z * (-1.6666654611e-1 + z * (8.3321608736e-3 + z * -1.9515295891e-4))
    cos_x = (1.0 - 0.5 * z) + z * z * (
        4.166664568298827e-2 + z * (-1.388731625493765e-3 + z * 2.443315711809948e-5)
    )
    swap = (quarter & 1) == 1
    cos_sign = jnp.where(((quarter + 1) & 2) == 2, -tapers, tapers)
    sin_sign = jnp.where((quarter & 2) == 2, -tapers, tapers)
    cosine = cos_sign * jnp.where(swap, sin_x, cos_x)
    sine = sin_sign * jnp.where(swap, cos_x, sin_x)
    return cosine, sine


def split_bf16(x):
    high = x.astype(jnp.bfloat16)
    return high, (x - high.astype(jnp.float32)).astype(jnp.bfloat16)


def dot32(a, b):
    return jnp.dot(a, b, preferred_element_type=jnp.float32)


def twice(x):
    return jnp.concatenate([x, x], axis=1)


def fused_kernel(
    slabs, n_band, traces, start_ref, taper_ref, weight_ref, fault_ref,
    t32, tb, start_at, taper_at, weight_at,
    waves, power, field, packed, halo, corner, prods_0, prods_1, part_out, part_in,
    load_sem, small_sem, main_send, main_recv, left_send, left_recv, right_send, right_recv,
    cross_send, cross_recv, cross_left_send, cross_left_recv, cross_right_send,
    cross_right_recv, part_send, part_recv, far_in,
):
    group = lax.axis_index("groups")
    beta = lax.axis_index("band")
    n_xl = lax.axis_size("xl")
    inl = lax.axis_index("inl")
    core = lax.axis_index("xl")
    slab = inl * n_xl + core
    il_rows, xl_cols = traces.shape[0], traces.shape[1]
    rows = il_rows * xl_cols

    def device(band_at, slab_at):
        return (group, band_at, slab_at // n_xl, slab_at % n_xl)

    smalls = [
        pltpu.make_async_copy(source, to, small_sem.at[i])
        for i, (source, to) in enumerate(
            (
                (start_ref, start_at),
                (taper_ref, taper_at),
                (weight_ref, weight_at),
            )
        )
    ]
    for small in smalls:
        small.start()
    loads = [
        pltpu.make_async_copy(
            traces.at[:, :, pl.ds(i * CHUNK, CHUNK)],
            t32.at[:, :, pl.ds(i * CHUNK, CHUNK)],
            load_sem.at[i],
        )
        for i in range(traces.shape[2] // CHUNK)
    ]
    for load in loads:
        load.start()

    barrier = pltpu.get_barrier_semaphore()
    for to_band in range(n_band):
        for ds in range(slabs):
            @pl.when((to_band >= beta - 1) & ((to_band != beta) | (ds > 0)))
            def _(to_band=to_band, ds=ds):
                pl.semaphore_signal(
                    barrier,
                    inc=1,
                    device_id=device(to_band, (slab + ds) % slabs),
                    device_id_type=MESH,
                )

    entered = jnp.minimum(beta + 2, n_band) * slabs - 1

    field[0:2, 3 + 9 * inl] = jnp.zeros((2,) + field.shape[2:], field.dtype)
    @pl.when(beta == 0)
    def _():
        halo[:, :, 0] = jnp.zeros((2, n_xl) + halo.shape[3:], halo.dtype)
        corner[:, 0] = jnp.zeros((2,) + corner.shape[2:], corner.dtype)

    @pl.when(beta == n_band - 1)
    def _():
        halo[:, :, 1] = jnp.zeros((2, n_xl) + halo.shape[3:], halo.dtype)
        corner[:, 1] = jnp.zeros((2,) + corner.shape[2:], corner.dtype)

    prods = (prods_0, prods_1)
    for half in range(2):
        for row in range(2):
            prods[half][:, 2 + row + 10 * inl] = jnp.zeros((3,) + prods_0.shape[2:], jnp.float32)

    half_r = lax.broadcasted_iota(jnp.int32, (2 * NB, 2 * NB), 0) // NB
    half_c = lax.broadcasted_iota(jnp.int32, (2 * NB, 2 * NB), 1) // NB
    mean_mat = jnp.where(half_r == half_c, 1.0 / NB, 0.0).astype(jnp.bfloat16)

    mean_mat = jnp.concatenate([mean_mat, mean_mat], axis=0)
    def one_hot(ones):
        return jnp.where(ones, 1.0, 0.0).astype(jnp.bfloat16)

    out_at = lax.broadcasted_iota(jnp.int32, (96, 8 * EDGE), 0)
    in_at = lax.broadcasted_iota(jnp.int32, (96, 8 * EDGE), 1)
    from_right = in_at // (4 * EDGE)
    in_row = in_at % (4 * EDGE) // EDGE
    in_col = in_at % EDGE - from_right * (EDGE - HALO)
    in_code = jnp.where(
        (in_col >= 0) & (in_col < HALO), from_right * 64 + in_row * HALO + in_col, -2
    )
    corner_code = jnp.where(
        out_at % 16 < 3 * HALO, out_at // 16 % 2 * 64 + out_at % 16 + (1 - inl) * HALO, -1
    )
    out_code = jnp.where(out_at < 64, out_at // 32 * 64 + out_at % 32, corner_code)
    pack_mat = one_hot(in_code == out_code)

    def column_of(place):
        near = jnp.where(place < xl_cols + RAD_XL, place - xl_cols - RAD_XL, place - RAD_XL)
        far = jnp.where(
            place < xl_cols + 2 * RAD_XL + 2,
            jnp.where(place == xl_cols + 2 * RAD_XL, -HALO, xl_cols + RAD_XL),
            4 * xl_cols,
        )
        return jnp.where(
            place < xl_cols, place, jnp.where(place < xl_cols + 2 * RAD_XL, near, far)
        )

    def unpack_matrix(depth, first):
        to = lax.broadcasted_iota(jnp.int32, (4 * EDGE, 2 * depth), 0)
        at = lax.broadcasted_iota(jnp.int32, (4 * EDGE, 2 * depth), 1)
        column = column_of(xl_cols + to % EDGE)
        row = to // EDGE - first
        west = (at < depth) & (column < 0) & (at == row * HALO + column + HALO)
        east = (at >= depth) & (column < 2 * xl_cols) & (
            at - depth == row * HALO + column - xl_cols
        )
        fits = (row >= 0) & (row < 4)
        return one_hot(fits & (west | ((column >= xl_cols) & east)))

    unpack_mat = unpack_matrix(32, 0)
    unpack_corner = unpack_matrix(16, inl)

    wide = xl_cols + 2 * RAD_XL
    cells = pl.ds(0, wide)
    shape = (wide, xl_cols + EDGE)
    out_x = column_of(lax.broadcasted_iota(jnp.int32, shape, 0))
    in_x = column_of(lax.broadcasted_iota(jnp.int32, shape, 1))
    diff_mat = (
        (in_x == out_x + 1).astype(jnp.float32) - (in_x == out_x - 1).astype(jnp.float32)
    ).astype(jnp.bfloat16)
    out_x = lax.broadcasted_iota(jnp.int32, (xl_cols, wide), 0)
    in_x = column_of(lax.broadcasted_iota(jnp.int32, (xl_cols, wide), 1))
    at_x = in_x + beta * xl_cols
    near = (jnp.abs(in_x - out_x) <= RAD_XL) & (at_x >= 0) & (at_x < xl_cols * n_band)
    box_mat = near.astype(jnp.float32)
    box_mats = [box_mat.astype(jnp.bfloat16), (2.0 * box_mat).astype(jnp.bfloat16)]
    for small in smalls:
        small.wait()
    start = twice(start_at[...])
    taper = twice(taper_at[...])
    early = lax.broadcasted_iota(jnp.int32, (HOP, 2 * NB), 1) < NB
    last = [jnp.zeros((HOP, 2 * NB), jnp.float32)] * 2
    for first in range(0, 512, 2 * HOP):
        now = wave_block(first, start, taper, HOP)
        for i in range(2):
            lanes = slice(i * 2 * NB, (i + 1) * 2 * NB)
            waves[first : first + HOP, lanes] = jnp.where(early, now[i], last[i]).astype(
                jnp.bfloat16
            )
            waves[first + HOP : first + 2 * HOP, lanes] = pltpu.roll(now[i], NB, 1).astype(
                jnp.bfloat16
            )
        last = now
    samples = traces.shape[2]
    tb[:, samples:] = jnp.zeros((rows, 128), jnp.bfloat16)

    def land(chunk):
        loads[chunk].wait()
        span = slice(chunk * CHUNK, (chunk + 1) * CHUNK)
        tb[:, span] = t32[:, :, span].reshape(rows, CHUNK).astype(jnp.bfloat16)

    def one_step(step):
        if step % 4 == 1 and step < 13:
            land(step // 4 + 1)
        at = step * 128
        coeffs = dot32(tb[:, pl.ds(at, 512)], waves[...])
        cosine, sine = coeffs[:, 0 : 2 * NB], coeffs[:, 2 * NB :]
        power[step] = cosine * cosine + sine * sine

    land(0)

    first_step = start >> 7
    def concentrations(m, slot):
        for j in range(2):
            pair = m * 2 + j
            chosen = power[pair]
            for q in range(1, 7):
                chosen = jnp.where(first_step == q, power[pair + q], chosen)
            amplitude = jnp.log(1.0 + chosen)
            average = dot32(jnp.concatenate(split_bf16(amplitude), axis=1), mean_mat)
            value = (amplitude / (1.0 + average)).astype(jnp.bfloat16)
            field[slot, mine, middle, j * 2 * NB : (j + 1) * 2 * NB] = value.reshape(
                il_rows, xl_cols, 2 * NB
            )

    mine = pl.ds(4 + core * il_rows, il_rows)
    border_from = pl.ds(4 + core * il_rows + 1 - inl, 3)
    border_to = pl.ds(1 + 11 * inl, 3)
    at_border = core == 1 - inl
    middle = pl.ds(0, xl_cols)
    first_cols, last_cols = pl.ds(0, EDGE), pl.ds(xl_cols - EDGE, EDGE)
    left_band, right_band = (beta + n_band - 1) % n_band, (beta + 1) % n_band
    has_left, has_right = beta > 0, beta < n_band - 1

    def place_of(m):
        owner, half = m % 2, m // 2
        return owner, half, half + 2 * ((core + owner) % 2)

    def pack(m):
        _, _, slot = place_of(m)
        edges = jnp.concatenate(
            [
                field[slot, mine, first_cols].reshape(4 * EDGE, 4 * NB),
                field[slot, mine, last_cols].reshape(4 * EDGE, 4 * NB),
            ],
            axis=0,
        )
        packed[m] = dot32(pack_mat, edges).astype(jnp.bfloat16)

    def unpack(half, block, halves, matrix):
        edges = dot32(matrix, halves).astype(jnp.bfloat16)
        field[half, pl.ds(4 * block, 4), pl.ds(xl_cols, EDGE)] = edges.reshape(4, EDGE, 4 * NB)

    sent = []

    def send(asked, source, to, send_sem, recv_sem, band_at, slab_at):
        copy = pltpu.make_async_remote_copy(
            src_ref=source,
            dst_ref=to,
            send_sem=send_sem,
            recv_sem=recv_sem,
            device_id=device(band_at, slab_at),
            device_id_type=MESH,
        )
        sent.append((asked, copy))

        @pl.when(asked)
        def _():
            copy.start()

    def send_rows(m):
        owner, half, slot = place_of(m)
        own_chip, other_chip = inl * n_xl + owner, (1 - inl) * n_xl + owner
        send(at_border, field.at[slot, border_from, middle], field.at[half, border_to, middle],
             cross_send.at[m], cross_recv.at[half], beta, other_chip)
        send(core == 1 - owner, field.at[slot, mine, middle], field.at[half, mine, middle],
             main_send.at[m], main_recv.at[half], beta, own_chip)

    def send_edges(m):
        owner, half, _ = place_of(m)
        own_chip, other_chip = inl * n_xl + owner, (1 - inl) * n_xl + owner
        send(has_left, packed.at[m, pl.ds(0, 32)], halo.at[half, core, 1],
             left_send.at[m], left_recv.at[half * 2 + core], left_band, own_chip)
        send(has_right, packed.at[m, pl.ds(32, 32)], halo.at[half, core, 0],
             right_send.at[m], right_recv.at[half * 2 + core], right_band, own_chip)
        send(at_border & has_left, packed.at[m, pl.ds(64, 16)], corner.at[half, 1],
             cross_left_send.at[m], cross_left_recv.at[half], left_band, other_chip)
        send(at_border & has_right, packed.at[m, pl.ds(80, 16)], corner.at[half, 0],
             cross_right_send.at[m], cross_right_recv.at[half], right_band, other_chip)

    for step in range(8):
        one_step(step)
    for m in range(4):
        for step in (range(0), range(8, 12), range(12, 14), range(0))[m]:
            one_step(step)
        concentrations(m, place_of(m)[2])
        if m == 0:
            pl.semaphore_wait(barrier, entered)

            send_rows(m)
        pack(m)
        if m:
            send_rows(m)
        send_edges(m)
        if m == 0:
            for to_band in range(n_band - 2):
                @pl.when(beta >= to_band + 2)
                def _(to_band=to_band):
                    for to_core in range(2):
                        pl.semaphore_signal(
                            far_in,
                            inc=1,
                            device_id=device(to_band, inl * n_xl + to_core),
                            device_id_type=MESH,
                        )

    weights = twice(twice(weight_at[...]))
    row = lax.broadcasted_iota(jnp.int32, (16, 4 * NB), 0)
    lane = lax.broadcasted_iota(jnp.int32, (16, 4 * NB), 1)
    w_high, w_low = split_bf16(weights)
    w_high = w_high.astype(jnp.float32)
    w_low = w_low.astype(jnp.float32)
    weight_mat = jnp.where(
        row == lane // NB, w_high, jnp.where(row - 4 == lane // NB, w_low, 0.0)
    ).astype(jnp.bfloat16)

    def landed(block, sem):
        pltpu.make_async_remote_copy(
            src_ref=block,
            dst_ref=block,
            send_sem=main_send.at[0],
            recv_sem=sem,
            device_id=device(beta, inl * n_xl + 1 - core),
            device_id_type=MESH,
        ).wait_recv()

    def own_chip_landed(half):
        landed(
            field.at[half, pl.ds(4 + (1 - core) * il_rows, il_rows), middle], main_recv.at[half]
        )

        @pl.when(has_right)
        def _():
            for source in range(2):
                landed(halo.at[half, source, 1], left_recv.at[half * 2 + source])

        @pl.when(has_left)
        def _():
            for source in range(2):
                landed(halo.at[half, source, 0], right_recv.at[half * 2 + source])

        for source in range(2):
            halves = jnp.concatenate([halo[half, source, 0], halo[half, source, 1]], axis=0)
            unpack(half, 1 + source, halves, unpack_mat)

    def other_chip_landed(half):
        landed(field.at[half, pl.ds(12 - 11 * inl, 3), middle], cross_recv.at[half])

        @pl.when(has_right)
        def _():
            landed(corner.at[half, 1], cross_left_recv.at[half])

        @pl.when(has_left)
        def _():
            landed(corner.at[half, 0], cross_right_recv.at[half])

        halves = jnp.concatenate([corner[half, 0], corner[half, 1]], axis=0)
        unpack(half, 3 - 3 * inl, halves, unpack_corner)

    def one_product(half, turn):
        i = 4 + turn + inl * (7 - 2 * turn)
        grad_xl = dot32(diff_mat, field[half, i])
        grad_in = field[half, i + 1, cells].astype(jnp.float32) - field[
            half, i - 1, cells
        ].astype(jnp.float32)
        prods[half][0, i] = grad_in * grad_in
        prods[half][1, i] = grad_in * grad_xl
        prods[half][2, i] = grad_xl * grad_xl

    parts = []

    def slab_scores(half, turn):
        place = turn + inl * (1 - 2 * turn)
        base = 2 + place * il_rows
        slot = turn * 2 + half
        sums = [[] for _ in range(il_rows)]
        for which in range(3):
            p = [prods[half][which, base + r] for r in range(8)]
            a, b, c = p[1] + p[2], p[5] + p[6], p[3] + p[4]
            ac, bc = a + c, b + c
            box = box_mats[which == 1]
            for r, total in enumerate((p[0] + ac, p[5] + ac, p[2] + bc, p[7] + bc)):
                high, low = split_bf16(total)
                sums[r].append(dot32(box, high) + dot32(box, low))
        scores = []
        for s_ii, s_ix, s_xx in sums:
            total = s_ii + s_xx + 4.0 * epsilon
            gap = s_ii - s_xx
            scores.append(1.0 - (gap * gap + s_ix * s_ix) / (total * total))
        high, low = split_bf16(jnp.concatenate(scores, axis=0))
        nt = (((1,), (1,)), ((), ()))
        both = lax.dot_general(
            weight_mat, high, nt, preferred_element_type=jnp.float32
        ) + lax.dot_general(weight_mat, low, nt, preferred_element_type=jnp.float32)
        both = both[0:8]
        both = both + pltpu.roll(both, 4, 0)
        upper = lax.broadcasted_iota(jnp.int32, (8, 128), 0) < 4
        part_out[slot] = jnp.where(upper, both[:, 0:128], both[:, 128:256])
        part = pltpu.make_async_remote_copy(
            src_ref=part_out.at[slot],
            dst_ref=part_in.at[beta],
            send_sem=part_send.at[slot],
            recv_sem=part_recv.at[beta],
            device_id=device(half * 2 + core, inl * n_xl + place),
            device_id_type=MESH,
        )
        own = (half * 2 + core == beta) & (place == core)
        parts.append((part, own))

        @pl.when(own)
        def _():
            part_in[beta] = part_out[slot]

        @pl.when(jnp.logical_not(own))
        def _():
            part.start()

    for half in range(2):
        if half == 0:
            @pl.when(beta < n_band - 2)
            def _():
                pl.semaphore_wait(far_in, (n_band - 2 - beta) * 2)

        own_chip_landed(half)
        for turn in range(7):
            one_product(half, turn)
        slab_scores(half, 0)
        other_chip_landed(half)
        for turn in range(7, 10):
            one_product(half, turn)
        slab_scores(half, 1)

    for asked, copy in sent:
        @pl.when(asked)
        def _(copy=copy):
            copy.wait_send()

    for source in range(n_band):
        @pl.when(jnp.logical_not((beta % 2 == core) & (beta == source)))
        def _(source=source):
            pltpu.make_async_remote_copy(
                src_ref=part_out.at[0],
                dst_ref=part_in.at[source],
                send_sem=part_send.at[0],
                recv_sem=part_recv.at[source],
                device_id=device((beta + 1) % n_band, slab),
                device_id_type=MESH,
            ).wait_recv()

    for source in range(n_band):
        fault_ref[source] = part_in[source]

    for part, own in parts:
        @pl.when(jnp.logical_not(own))
        def _(part=part):
            part.wait_send()


def final_kernel(parts_ref, labels_ref, fault_ref, misfit_ref):
    first_half = lax.broadcasted_iota(jnp.int32, (8, 128), 1) < 64
    labels = labels_ref[...].astype(jnp.float32)
    halves = [[], []]
    for c in range(0, parts_ref.shape[0], 2):
        one, two = parts_ref[c], parts_ref[c + 1]
        halves[0].append(jnp.where(first_half, one, pltpu.roll(two, 64, 1)))
        halves[1].append(jnp.where(first_half, pltpu.roll(one, 64, 1), two))
    frames = fault_ref.shape[0]
    for odd in range(2):
        blocks = jnp.concatenate(halves[odd], axis=1)
        for two in range(2):
            i = two * 2 + odd
            here = blocks[two * 4 : two * 4 + 4]
            miss = jnp.tanh(here) - labels[i : i + 1]
            miss = miss * miss
            for f in range(frames):
                fault_ref[f, i : i + 1] = here[f : f + 1]
                misfit_ref[f, i : i + 1] = miss[f : f + 1]


def fused(traces, band_start, taper_len, band_weight, labels):
    il_rows, xl_cols, samples = traces.shape
    rows = il_rows * xl_cols
    n_band = lax.axis_size("band")
    slabs = lax.axis_size("inl") * lax.axis_size("xl")
    frames = FR // n_band
    out = jax.ShapeDtypeStruct((frames, il_rows, xl_cols * n_band), jnp.float32)
    vmem = pl.BlockSpec(memory_space=pltpu.VMEM)
    dma = pltpu.SemaphoreType.DMA
    parts = pl.pallas_call(
        functools.partial(fused_kernel, slabs, n_band),
        out_shape=jax.ShapeDtypeStruct((n_band, 8, 128), jnp.float32),
        in_specs=[pl.BlockSpec(memory_space=pltpu.HBM)] * 4,
        out_specs=vmem,
        scratch_shapes=[
            pltpu.VMEM((il_rows, xl_cols, samples), jnp.float32),
            pltpu.VMEM((rows, samples + 128), jnp.bfloat16),
            pltpu.VMEM((1, NB), jnp.int32),
            pltpu.VMEM((1, NB), jnp.int32),
            pltpu.VMEM((1, NB), jnp.float32),
            pltpu.VMEM((512, 4 * NB), jnp.bfloat16),
            pltpu.VMEM((14, rows, 2 * NB), jnp.float32),
            pltpu.VMEM((4, 16, xl_cols + EDGE, 4 * NB), jnp.bfloat16),
            pltpu.VMEM((4, 96, 4 * NB), jnp.bfloat16),
            pltpu.VMEM((2, 2, 2, 32, 4 * NB), jnp.bfloat16),
            pltpu.VMEM((2, 2, 16, 4 * NB), jnp.bfloat16),
            pltpu.VMEM((3, 16, xl_cols + 2 * RAD_XL, 4 * NB), jnp.float32),
            pltpu.VMEM((3, 16, xl_cols + 2 * RAD_XL, 4 * NB), jnp.float32),
            pltpu.VMEM((slabs, 8, 128), jnp.float32),
            pltpu.VMEM((n_band, 8, 128), jnp.float32),
            dma((samples // CHUNK,)),
            dma((3,)),
            dma((4,)),
            dma((2,)),
            dma((4,)),
            dma((4,)),
            dma((4,)),
            dma((4,)),
            dma((4,)),
            dma((2,)),
            dma((4,)),
            dma((2,)),
            dma((4,)),
            dma((2,)),
            dma((slabs,)),
            dma((n_band,)),
            pltpu.SemaphoreType.REGULAR,
        ],
        compiler_params=pltpu.CompilerParams(
            collective_id=0, has_side_effects=True, vmem_limit_bytes=32 * 1024 * 1024
        ),
    )(
        *[
            pltpu.with_memory_space_constraint(operand, pltpu.HBM)
            for operand in (
                traces,
                band_start.reshape(1, NB),
                taper_len.reshape(1, NB),
                band_weight.reshape(1, NB),
            )
        ]
    )
    return pl.pallas_call(
        final_kernel, out_shape=(out, out), in_specs=[vmem, vmem], out_specs=(vmem, vmem)
    )(
        pltpu.with_memory_space_constraint(parts, pltpu.VMEM),
        pltpu.with_memory_space_constraint(labels, pltpu.VMEM),
    )


def solution(mesh):
    shape = mesh.shape
    square = shape["band"] == 4 and shape["inl"] == 2 and shape["xl"] == 2
    return jax.shard_map(
        fused if square else on_device,
        mesh=mesh,
        in_specs=(
            P(("groups", "inl", "xl"), "band", None),
            P(),
            P(),
            P(),
            P(("groups", "inl", "xl"), None),
        ),
        out_specs=(
            P(("groups", "band"), ("inl", "xl"), None),
            P(("groups", "band"), ("inl", "xl"), None),
        ),
        check_vma=False,
    )
```
